32 devices in a mesh: ia: 2 (over x), ja: 4 (over y, core), ka: 4 (over z).
Axes of the slice: x: 2, y: 2, z: 4, core: 2. Of those that a mesh axis runs over, the one named last changes fastest.
Arguments:
- tensor: bfloat16 [512, 512, 512], P('ia', 'ja', 'ka'), may hold values from 0 to 122880
- matrix: bfloat16 [512, 32768], P(None, ('ia', 'ja', 'ka')), may hold values from 0 to 4096000
- first_factor: bfloat16 [512, 256], P('ia'), may hold values from 0.05 to 2
- second_factor: bfloat16 [512, 256], P('ja'), may hold values from 0.05 to 2
- time_factor: bfloat16 [512, 256], P('ka'), may hold values from 0.05 to 2
- column_factor: bfloat16 [32768, 256], P(('ia', 'ja', 'ka')), may hold values from 0.05 to 2
Outputs:
- first_new: bfloat16 [512, 256], P('ia')
- second_new: bfloat16 [512, 256], P('ja')
- time_new: bfloat16 [512, 256], P('ka')
The draws below stay inside these ranges and needn't reach their ends.
All inputs are finite; a program needn't handle non-finite values.
Results may differ from the reference program's by a relative error of at most 0.00075.
The reference program's roundings to bfloat16 on the way (of `khatri`) count: a program that leaves them out, or rounds other values in their place, can miss the bound.
Values may be sent and summed in bfloat16 or wider, within the bound.
No kernel may reach another device: no remote copies, remote signals or barrier semaphores. Data moves between devices by JAX's collectives and lax.ppermute only.
A program may use at most 128 MiB of HBM per device.

```python
import jax
import jax.numpy as jnp
from jax import lax

R = 256
I_DEV = 256
M_DEV = 1024
I = 512
J = 512
K = 512
M = 32768


component_count = 512


def drawn_members(key):
    member_key = jax.random.fold_in(key, 41)
    key_list = jax.random.split(member_key, 2)
    members = jax.random.randint(key_list[0], (I, 2), 0, component_count)
    weights = jnp.exp(jax.random.uniform(key_list[1], (I, 2), jnp.float32, -0.7, 0.7))
    return (members, weights)


def peaked_columns(key, length, fraction):
    key_list = jax.random.split(key, 2)
    support = (jax.random.uniform(key_list[0], (length, component_count), jnp.float32, 0.0, 1.0) < fraction).astype(jnp.float32)
    return support * jnp.exp(jax.random.uniform(key_list[1], (length, component_count), jnp.float32, -0.7, 0.7))


def draw_tensor(key, part):
    members, weights = drawn_members(key)
    key_list = jax.random.split(jax.random.fold_in(key, 3), 3)
    plane_columns = peaked_columns(key_list[0], J, 0.0625)
    time_columns = peaked_columns(key_list[1], K, 0.0625)
    plane_rows = plane_columns.T[members] * weights[:, :, None]
    time_rows = time_columns.T[members]
    planted = jnp.einsum('isj,isk->ijk', plane_rows, time_rows)
    noise = jax.random.uniform(key_list[2], (I, J, K), jnp.float32, 0.0, 1.0)
    mass = jnp.minimum(noise + 128.0 * planted, 960.0)
    return (0.5 * R * mass).astype(jnp.bfloat16)


def draw_matrix(key, part):
    key_list = jax.random.split(jax.random.fold_in(key, 5), 3)
    blocks_total = M // M_DEV
    row_span = I // blocks_total
    pairing = jax.random.permutation(key_list[0], blocks_total)
    row_owner = pairing[jnp.arange(I) // row_span]
    column_block = jnp.arange(M) // M_DEV
    paired = (row_owner[:, None] == column_block[None, :]).astype(jnp.float32)
    heavy = jnp.exp(3.5 * jax.random.normal(key_list[1], (I, M), jnp.float32))
    spread = jax.random.uniform(key_list[2], (I, M), jnp.float32, 0.5, 1.5)
    mass = heavy + paired * (48.0 * blocks_total) * spread
    size_scale = R * J * K / (100.0 * M)
    ceiling = 2000.0 * R * J * K / M
    return jnp.minimum(mass * size_scale, ceiling).astype(jnp.bfloat16)


def level_scale(key, row_count):
    levels = jax.random.uniform(key, (8, 8), jnp.float32, -1.1, 0.9)
    row_block = jnp.arange(row_count) * 8 // row_count
    rank_block = jnp.arange(R) * 8 // R
    return jnp.exp(levels[row_block][:, rank_block])


def level_factor(key, row_count):
    key_list = jax.random.split(key, 2)
    scale = level_scale(key_list[0], row_count)
    base = jax.random.uniform(key_list[1], (row_count, R), jnp.float32, 0.4, 1.4)
    return jnp.clip(base * scale, 0.05, 2.0).astype(jnp.bfloat16)


def draw_first_factor(key, part):
    return level_factor(jax.random.fold_in(key, 61), I)


def draw_second_factor(key, part):
    return level_factor(jax.random.fold_in(key, 67), J)


def draw_time_factor(key, part):
    return level_factor(jax.random.fold_in(key, 71), K)


def draw_column_factor(key, part):
    key_list = jax.random.split(jax.random.fold_in(key, 73), 2)
    scale = level_scale(key_list[0], M)
    base = jnp.exp(jax.random.uniform(key_list[1], (M, R), jnp.float32, -1.8971, 0.4055))
    return jnp.clip(base * scale, 0.05, 2.0).astype(jnp.bfloat16)


def setup_inputs(seed: int = 0) -> dict:
    streams_of = jax.random.split(jax.random.key(seed), 7)
    return {
        "tensor": draw_tensor(jax.random.fold_in(streams_of[6], 71), 0),
        "matrix": draw_matrix(jax.random.fold_in(streams_of[6], 71), 0),
        "first_factor": draw_first_factor(jax.random.fold_in(streams_of[6], 71), 0),
        "second_factor": draw_second_factor(jax.random.fold_in(streams_of[6], 71), 0),
        "time_factor": draw_time_factor(jax.random.fold_in(streams_of[6], 71), 0),
        "column_factor": draw_column_factor(jax.random.fold_in(streams_of[6], 71), 0),
    }


def cross_product(values):
    return jnp.dot(values.T, values, preferred_element_type=jnp.float32)


def rescale(factor, numerator, gram_total):
    widened = factor.astype(jnp.float32)
    denominator = jnp.dot(widened, gram_total, precision=lax.Precision.HIGHEST)
    return (widened * numerator / denominator).astype(jnp.bfloat16)


def reference(tensor, matrix, first_factor, second_factor, time_factor, column_factor):
    gram_second = cross_product(second_factor)
    gram_time = cross_product(time_factor)
    gram_column = cross_product(column_factor)
    khatri = (second_factor.astype(jnp.float32)[:, None, :] * time_factor.astype(jnp.float32)[None, :, :]).astype(jnp.bfloat16).reshape(J * K, R)
    blocked = tensor.reshape(I // I_DEV, I_DEV, J * K)

    def slab_block(tile_rows):
        return jnp.dot(tile_rows, khatri, preferred_element_type=jnp.float32)

    slab = lax.map(slab_block, blocked).reshape(I, R)

    def add_columns(step, total):
        start = (step * M_DEV).astype(jnp.int32)
        columns = lax.dynamic_slice_in_dim(matrix, start, M_DEV, 1)
        factor_rows = lax.dynamic_slice_in_dim(column_factor, start, M_DEV, 0)
        return total + jnp.dot(columns, factor_rows, preferred_element_type=jnp.float32)

    coupled = lax.fori_loop(0, M // M_DEV, add_columns, jnp.zeros((I, R), jnp.float32))
    first_new = rescale(first_factor, slab + coupled, gram_second * gram_time + gram_column)

    def add_weighted(step, total):
        start = (step * I_DEV).astype(jnp.int32)
        tile_rows = lax.dynamic_slice_in_dim(tensor, start, I_DEV, 0)
        factor_rows = lax.dynamic_slice_in_dim(first_new, start, I_DEV, 0)
        return total + lax.dot_general(tile_rows, factor_rows, (((0,), (0,)), ((), ())), preferred_element_type=jnp.float32)

    weighted = lax.fori_loop(0, I // I_DEV, add_weighted, jnp.zeros((J, K, R), jnp.float32))
    plane_sum = jnp.sum(weighted * time_factor.astype(jnp.float32)[None, :, :], axis=1)
    gram_first = cross_product(first_new)
    second_new = rescale(second_factor, plane_sum, gram_first * gram_time)
    time_sum = jnp.sum(weighted * second_new.astype(jnp.float32)[:, None, :], axis=0)
    gram_new = cross_product(second_new)
    time_new = rescale(time_factor, time_sum, gram_first * gram_new)
    return (first_new, second_new, time_new)
```

```python
import functools

import jax
import jax.numpy as jnp
from jax import lax
from jax.sharding import PartitionSpec as P


def cross_product(values):
    return lax.dot_general(
        values, values, (((0,), (0,)), ((), ())), preferred_element_type=jnp.float32
    )


def swap(values, axis, size, mask):
    return lax.ppermute(values, axis, [(i, i ^ mask) for i in range(size)])


def halve(values, axis, size, mask):
    half = values.shape[0] // 2
    bit = (lax.axis_index(axis) & mask) // mask
    kept = lax.dynamic_slice_in_dim(values, bit * half, half, 0)
    sent = lax.dynamic_slice_in_dim(values, (1 - bit) * half, half, 0)
    return kept + swap(sent, axis, size, mask)


def double(values, axis, size, mask):
    other = swap(values, axis, size, mask)
    bit = (lax.axis_index(axis) & mask) // mask
    return jnp.where(
        bit == 0,
        jnp.concatenate([values, other], 0),
        jnp.concatenate([other, values], 0),
    )


def tree_sum(terms):
    while len(terms) > 1:
        terms = [terms[i] + terms[i + 1] for i in range(0, len(terms), 2)]
    return terms[0]


def masks_of(size):
    return [1 << b for b in range(size.bit_length() - 1)]


def spread(values, axis, size, step=1):
    return [values] + [swap(values, axis, size, d) for d in range(step, size, step)]


def all_sum(values, axis, size, step=1):
    return tree_sum(spread(values, axis, size, step))


def full_dot(left, right, dims):
    return lax.dot_general(
        left, right, (dims, ((), ())), precision=lax.Precision.HIGHEST,
        preferred_element_type=jnp.float32,
    )


def on_device(
    size_i, size_j, size_k, tensor, matrix, first_factor, second_factor, time_factor, column_factor
):
    f32 = jnp.float32
    tile_i, tile_j, tile_k = tensor.shape
    rank = first_factor.shape[1]

    gram_column = cross_product(column_factor)
    gram_second = cross_product(second_factor)
    grams = jnp.concatenate([gram_column, gram_second], 1)
    for mask in masks_of(size_j):
        grams = halve(grams, "ja", size_j, mask)
    gram_column, gram_second = grams[:, :rank], grams[:, rank:]
    gram_column = all_sum(gram_column, "ka", size_k)
    gram_column = all_sum(gram_column, "ia", size_i)
    gram_time = tree_sum([cross_product(piece) for piece in spread(time_factor, "ka", size_k)])
    share = rank // size_j
    part = 0
    for mask in masks_of(size_j):
        part = 2 * part + (lax.axis_index("ja") & mask) // mask
    gram_time_rows = lax.dynamic_slice_in_dim(gram_time, part * share, share, 0)
    gram_total = gram_second * gram_time_rows + gram_column
    first_wide = first_factor.astype(f32)
    denominator = full_dot(gram_total, first_wide, ((1,), (1,)))

    coupled = jnp.dot(matrix, column_factor, preferred_element_type=f32)
    for mask in reversed(masks_of(size_i)):
        coupled = halve(coupled, "ia", size_i, mask)
    khatri = (
        (second_factor.astype(f32)[:, None, :] * time_factor.astype(f32)[None, :, :])
        .astype(jnp.bfloat16)
        .reshape(tile_j * tile_k, rank)
    )
    slab = jnp.dot(
        tensor.reshape(tile_i, tile_j * tile_k), khatri, preferred_element_type=f32
    )
    numerator = (slab + coupled).T
    for mask in masks_of(size_j):
        numerator = halve(numerator, "ja", size_j, mask)
    numerator = all_sum(numerator, "ka", size_k)
    own = lax.dynamic_slice_in_dim(first_wide.T, part * share, share, 0)
    first_new = (own * numerator / denominator).astype(jnp.bfloat16)
    for mask in reversed(masks_of(size_j)):
        first_new = double(first_new, "ja", size_j, mask)
    first_new = first_new.T

    gram_first = tree_sum([cross_product(piece) for piece in spread(first_new, "ia", size_i)])
    weighted = lax.dot_general(
        tensor, first_new, (((0,), (0,)), ((), ())), preferred_element_type=f32
    )
    plane_sum = jnp.sum(weighted * time_factor.astype(f32)[None, :, :], axis=1)
    for mask in reversed(masks_of(size_i)):
        plane_sum = halve(plane_sum, "ia", size_i, mask)
    plane_sum = all_sum(plane_sum, "ka", size_k)
    rows = tile_j // size_i
    own = lax.dynamic_slice_in_dim(second_factor, lax.axis_index("ia") * rows, rows, 0).astype(f32)
    denominator = full_dot(own, gram_first * gram_time, ((1,), (0,)))
    second_new = (own * plane_sum / denominator).astype(jnp.bfloat16)
    for mask in masks_of(size_i):
        second_new = double(second_new, "ia", size_i, mask)

    gram_new = tree_sum([cross_product(piece) for piece in spread(second_new, "ja", size_j)])
    time_sum = jnp.sum(weighted * second_new.astype(f32)[:, None, :], axis=0)
    time_sum = halve(time_sum, "ja", size_j, 1)
    time_sum = all_sum(time_sum, "ja", size_j, 2)
    time_sum = all_sum(time_sum, "ia", size_i)
    rows = tile_k // 2
    own = lax.dynamic_slice_in_dim(
        time_factor, (lax.axis_index("ja") % 2) * rows, rows, 0
    ).astype(f32)
    denominator = full_dot(own, gram_first * gram_new, ((1,), (0,)))
    time_new = (own * time_sum / denominator).astype(jnp.bfloat16)
    time_new = double(time_new, "ja", size_j, 1)
    return (first_new, second_new, time_new)


def solution(mesh):
    sizes = (mesh.shape["ia"], mesh.shape["ja"], mesh.shape["ka"])
    return jax.shard_map(
        functools.partial(on_device, *sizes),
        mesh=mesh,
        in_specs=(
            P("ia", "ja", "ka"),
            P(None, ("ia", "ja", "ka")),
            P("ia", None),
            P("ja", None),
            P("ka", None),
            P(("ia", "ja", "ka"), None),
        ),
        out_specs=(P("ia", None), P("ja", None), P("ka", None)),
        check_vma=False,
    )
```

```python
import functools

import jax
import jax.numpy as jnp
from jax import lax
from jax.experimental import pallas as pl
from jax.experimental.pallas import tpu as pltpu
from jax.sharding import PartitionSpec as P


ANY = pl.BlockSpec(memory_space=pl.ANY)
VMEM = pl.BlockSpec(memory_space=pltpu.VMEM)
MIB = 1 << 20


def chunk_of(length, most):
    size = min(length, most)
    while length % size:
        size //= 2
    return size


def kernel_call(kernel, flops, nbytes, limit, **kwargs):
    return pl.pallas_call(
        kernel,
        cost_estimate=pl.CostEstimate(flops=flops, bytes_accessed=nbytes, transcendentals=0),
        compiler_params=pltpu.CompilerParams(vmem_limit_bytes=limit),
        **kwargs,
    )


def slab_kernel(first, count, chunk, tensor, second, time, *refs):
    *starts, total, planes, read, read_sem, swapped, write_sem = refs
    steps = count // chunk

    def fetch(step):
        source = tensor.at[:, pl.ds(first + step * chunk, chunk)]
        return pltpu.make_async_copy(source, read.at[step], read_sem.at[step])

    def put(step):
        target = planes.at[pl.ds(step * chunk, chunk)]
        return pltpu.make_async_copy(swapped.at[step], target, write_sem.at[step])

    for step in range(steps):
        fetch(step).start()
    time_wide = time[...].astype(jnp.float32)
    total[...] = starts[0][...] + starts[1][...] if starts else jnp.zeros_like(total)

    def body(step, carry):
        fetch(step).wait()
        block = jnp.swapaxes(read[step], 0, 1)
        swapped[step] = block
        put(step).start()
        row = pl.multiple_of(first + step * chunk, chunk)
        weights = second[pl.ds(row, chunk), :].astype(jnp.float32)
        khatri = jnp.concatenate(
            [(weights[j : j + 1, :] * time_wide).astype(jnp.bfloat16) for j in range(chunk)], 0
        )
        tiles = jnp.concatenate([block[j] for j in range(chunk)], 1)
        total[...] += jnp.dot(tiles, khatri, preferred_element_type=jnp.float32)
        return carry

    lax.fori_loop(0, steps, body, 0)
    if starts:
        total[...] = total[...].T

    def finish(step, carry):
        put(step).wait()
        return carry

    lax.fori_loop(0, steps, finish, 0)


def slab_part(tensor, second, time, first, count, starts=()):
    tile_i, _, tile_k = tensor.shape
    rank = time.shape[1]
    chunk = chunk_of(count, 16)
    steps = count // chunk
    args = (tensor, second, time) + tuple(starts)
    return kernel_call(
        functools.partial(slab_kernel, first, count, chunk),
        2 * tile_i * count * tile_k * rank,
        4 * tile_i * count * tile_k,
        60 * MIB,
        out_shape=(
            jax.ShapeDtypeStruct((tile_i, rank), jnp.float32),
            jax.ShapeDtypeStruct((count, tile_i, tile_k), tensor.dtype),
        ),
        in_specs=[ANY] + [VMEM] * (len(args) - 1),
        out_specs=(VMEM, ANY),
        scratch_shapes=[
            pltpu.VMEM((steps, tile_i, chunk, tile_k), tensor.dtype),
            pltpu.SemaphoreType.DMA((steps,)),
            pltpu.VMEM((steps, chunk, tile_i, tile_k), tensor.dtype),
            pltpu.SemaphoreType.DMA((steps,)),
        ],
    )(*args)


def turn_kernel(chunk, steps, parts, planes, turned, read, read_sem, ready, write_sem):
    def put(part, step):
        slot = part * steps + step
        target = turned.at[pl.ds(slot * chunk, chunk)]
        return pltpu.make_async_copy(ready.at[slot], target, write_sem.at[slot])

    def fetch(part, step):
        slot = part * steps + step
        source = planes[part].at[pl.ds(step * chunk, chunk)]
        return pltpu.make_async_copy(source, read.at[slot], read_sem.at[slot])

    for part in range(parts):
        for step in range(steps):
            fetch(part, step).start()
    for part in range(parts):

        def body(step, carry):
            fetch(part, step).wait()
            for j in range(chunk):
                ready[part * steps + step, j] = read[part * steps + step, j].T
            put(part, step).start()
            return carry

        lax.fori_loop(0, steps, body, 0)
    for part in range(parts):

        def finish(step, carry):
            put(part, step).wait()
            return carry

        lax.fori_loop(0, steps, finish, 0)


def turn(pieces):
    count, tile_i, tile_k = pieces[0].shape
    parts = len(pieces)
    chunk = chunk_of(count, 16)
    steps = count // chunk

    def kernel(*refs):
        turn_kernel(chunk, steps, parts, refs[:parts], *refs[parts:])

    return kernel_call(
        kernel,
        0,
        4 * parts * count * tile_i * tile_k,
        60 * MIB,
        out_shape=jax.ShapeDtypeStruct((parts * count, tile_k, tile_i), pieces[0].dtype),
        in_specs=[ANY] * parts,
        out_specs=ANY,
        scratch_shapes=[
            pltpu.VMEM((parts * steps, chunk, tile_i, tile_k), pieces[0].dtype),
            pltpu.SemaphoreType.DMA((parts * steps,)),
            pltpu.VMEM((parts * steps, chunk, tile_k, tile_i), pieces[0].dtype),
            pltpu.SemaphoreType.DMA((parts * steps,)),
        ],
    )(*pieces)


def weighted_kernel(chunk, steps, over_time, turned, first_turned, weights, total, read, read_sem):
    def fetch(step):
        source = turned.at[pl.ds(step * chunk, chunk)]
        return pltpu.make_async_copy(source, read.at[step], read_sem.at[step])

    for step in range(steps):
        fetch(step).start()
    shared = first_turned[...]
    if not over_time:
        total[...] = jnp.zeros_like(total)

    def body(step, carry):
        fetch(step).wait()
        sums = []
        for j in range(chunk):
            weighted = lax.dot_general(
                read[step, j], shared, (((1,), (1,)), ((), ())), preferred_element_type=jnp.float32
            )
            if over_time:
                sums.append(jnp.sum(weighted * weights[...], axis=0, keepdims=True))
            else:
                sums.append(weighted * weights[pl.ds(step * chunk + j, 1), :])
        if over_time:
            row = pl.multiple_of(step * chunk, chunk)
            total[pl.ds(row, chunk), :] = jnp.concatenate(sums, 0)
        else:
            part = total[...]
            for term in sums:
                part = part + term
            total[...] = part
        return carry

    lax.fori_loop(0, steps, body, 0)


def weighted_sum(turned, first_turned, weights, over_time):
    tile_j, tile_k, tile_i = turned.shape
    rank = first_turned.shape[0]
    chunk = chunk_of(tile_j, 16)
    steps = tile_j // chunk
    return kernel_call(
        functools.partial(weighted_kernel, chunk, steps, over_time),
        2 * tile_i * tile_j * tile_k * rank,
        2 * tile_i * tile_j * tile_k,
        60 * MIB,
        out_shape=jax.ShapeDtypeStruct((tile_j if over_time else tile_k, rank), jnp.float32),
        in_specs=[ANY, VMEM, VMEM],
        out_specs=VMEM,
        scratch_shapes=[
            pltpu.VMEM((steps, chunk, tile_k, tile_i), turned.dtype),
            pltpu.SemaphoreType.DMA((steps,)),
        ],
    )(turned, first_turned, weights)


def cross_product(values):
    return lax.dot_general(
        values, values, (((0,), (0,)), ((), ())), preferred_element_type=jnp.float32
    )


def row_product(values):
    return lax.dot_general(
        values, values, (((1,), (1,)), ((), ())), preferred_element_type=jnp.float32
    )


def swap(values, axis, size, mask):
    return lax.ppermute(values, axis, [(i, i ^ mask) for i in range(size)])


def halve(values, axis, size, mask):
    half = values.shape[0] // 2
    bit = (lax.axis_index(axis) & mask) // mask
    kept = lax.dynamic_slice_in_dim(values, bit * half, half, 0)
    sent = lax.dynamic_slice_in_dim(values, (1 - bit) * half, half, 0)
    return kept + swap(sent, axis, size, mask)


def double(values, axis, size, mask):
    other = swap(values, axis, size, mask)
    bit = (lax.axis_index(axis) & mask) // mask
    return jnp.where(
        bit == 0,
        jnp.concatenate([values, other], 0),
        jnp.concatenate([other, values], 0),
    )


def tree_sum(terms):
    while len(terms) > 1:
        terms = [terms[i] + terms[i + 1] for i in range(0, len(terms), 2)]
    return terms[0]


def masks_of(size):
    return [1 << b for b in range(size.bit_length() - 1)]


def spread(values, axis, size, step=1):
    return [values] + [swap(values, axis, size, d) for d in range(step, size, step)]


def all_sum(values, axis, size, step=1):
    return tree_sum(spread(values, axis, size, step))


def full_dot(left, right, dims):
    return lax.dot_general(
        left, right, (dims, ((), ())), precision=lax.Precision.HIGHEST,
        preferred_element_type=jnp.float32,
    )


def on_device(
    size_i, size_j, size_k, tensor, matrix, first_factor, second_factor, time_factor, column_factor
):
    f32 = jnp.float32
    _, tile_j, tile_k = tensor.shape
    rank = first_factor.shape[1]

    gram_column = cross_product(column_factor)
    gram_second = cross_product(second_factor)
    grams = jnp.concatenate([gram_column, gram_second], 1)
    for mask in masks_of(size_j):
        grams = halve(grams, "ja", size_j, mask)
    gram_column, gram_second = grams[:, :rank], grams[:, rank:]
    gram_column = all_sum(gram_column, "ka", size_k)
    gram_column = all_sum(gram_column, "ia", size_i)
    times = spread(time_factor, "ka", size_k)
    gram_time = tree_sum([cross_product(piece) for piece in times])
    share = rank // size_j
    part = 0
    for mask in masks_of(size_j):
        part = 2 * part + (lax.axis_index("ja") & mask) // mask
    gram_time_rows = lax.dynamic_slice_in_dim(gram_time, part * share, share, 0)
    gram_total = gram_second * gram_time_rows + gram_column
    first_wide = first_factor.astype(f32)
    denominator = full_dot(gram_total, first_wide, ((1,), (1,)))

    coupled = jnp.dot(matrix, column_factor, preferred_element_type=f32)
    for mask in reversed(masks_of(size_i)):
        coupled = halve(coupled, "ia", size_i, mask)
    half = tile_j // 2
    slab, low = slab_part(tensor, second_factor, time_factor, 0, half)
    numerator, high = slab_part(
        tensor, second_factor, time_factor, half, half, (slab, coupled)
    )
    for mask in masks_of(size_j):
        numerator = halve(numerator, "ja", size_j, mask)
    numerator = all_sum(numerator, "ka", size_k)
    own = lax.dynamic_slice_in_dim(first_wide.T, part * share, share, 0)
    first_new = (own * numerator / denominator).astype(jnp.bfloat16)
    for mask in reversed(masks_of(size_j)):
        first_new = double(first_new, "ja", size_j, mask)
    turned = turn((low, high))

    firsts = spread(first_new, "ia", size_i)
    gram_first = tree_sum([row_product(piece) for piece in firsts])
    plane_sum = weighted_sum(turned, first_new, time_factor.astype(f32), True)
    for mask in reversed(masks_of(size_i)):
        plane_sum = halve(plane_sum, "ia", size_i, mask)
    plane_sum = all_sum(plane_sum, "ka", size_k)
    rows = tile_j // size_i
    own = lax.dynamic_slice_in_dim(second_factor, lax.axis_index("ia") * rows, rows, 0).astype(f32)
    denominator = full_dot(own, gram_first * gram_time, ((1,), (0,)))
    second_new = (own * plane_sum / denominator).astype(jnp.bfloat16)
    for mask in masks_of(size_i):
        second_new = double(second_new, "ia", size_i, mask)

    seconds = spread(second_new, "ja", size_j)
    gram_new = tree_sum([cross_product(piece) for piece in seconds])
    time_sum = weighted_sum(turned, first_new, second_new.astype(f32), False)
    time_sum = halve(time_sum, "ja", size_j, 1)
    time_sum = all_sum(time_sum, "ja", size_j, 2)
    time_sum = all_sum(time_sum, "ia", size_i)
    rows = tile_k // 2
    own = lax.dynamic_slice_in_dim(
        time_factor, (lax.axis_index("ja") % 2) * rows, rows, 0
    ).astype(f32)
    denominator = full_dot(own, gram_first * gram_new, ((1,), (0,)))
    time_new = (own * time_sum / denominator).astype(jnp.bfloat16)
    time_new = double(time_new, "ja", size_j, 1)
    return (first_new.T, second_new, time_new)


def in_layer(sizes, *args):
    return on_device(*sizes, *args)


def solution(mesh):
    sizes = (mesh.shape["ia"], mesh.shape["ja"], mesh.shape["ka"])
    return jax.shard_map(
        functools.partial(in_layer, sizes),
        mesh=mesh,
        in_specs=(
            P("ia", "ja", "ka"),
            P(None, ("ia", "ja", "ka")),
            P("ia", None),
            P("ja", None),
            P("ka", None),
            P(("ia", "ja", "ka"), None),
        ),
        out_specs=(P("ia", None), P("ja", None), P("ka", None)),
        check_vma=False,
    )
```

```python
import functools

import jax
import jax.numpy as jnp
from jax import lax
from jax.experimental import pallas as pl
from jax.experimental.pallas import tpu as pltpu
from jax.sharding import PartitionSpec as P


ANY = pl.BlockSpec(memory_space=pl.ANY)
VMEM = pl.BlockSpec(memory_space=pltpu.VMEM)
LIMIT = 32 << 20


def in_hbm(values):
    return pltpu.with_memory_space_constraint(values, pltpu.HBM)


def chunk_of(length, most):
    size = min(length, most)
    while length % size:
        size //= 2
    return size


def kernel_call(kernel, flops, nbytes, **kwargs):
    return pl.pallas_call(
        kernel,
        cost_estimate=pl.CostEstimate(flops=flops, bytes_accessed=nbytes, transcendentals=0),
        compiler_params=pltpu.CompilerParams(vmem_limit_bytes=LIMIT),
        **kwargs,
    )


def local_kernel(matrix, column, second, time, coupled, grams, gram_time):
    f32 = jnp.float32
    rank = column.shape[1]
    turned = column[...].T
    grams[:, :rank] = jnp.dot(turned, column[...], preferred_element_type=f32)
    coupled[...] = lax.dot_general(
        turned, matrix[...], (((1,), (1,)), ((), ())), preferred_element_type=f32
    )
    grams[:, rank:] = jnp.dot(second[...].T, second[...], preferred_element_type=f32)
    gram_time[...] = jnp.dot(time[...].T, time[...], preferred_element_type=f32)


def local_products(matrix, column, second, time):
    rank = column.shape[1]
    rows, width = matrix.shape
    f32 = jnp.float32
    return kernel_call(
        local_kernel,
        2 * width * rank * (rows + rank),
        2 * width * (rows + rank),
        out_shape=(
            jax.ShapeDtypeStruct((rank, rows), f32),
            jax.ShapeDtypeStruct((rank, 2 * rank), f32),
            jax.ShapeDtypeStruct((rank, rank), f32),
        ),
        in_specs=[VMEM] * 4,
        out_specs=(VMEM,) * 3,
    )(matrix, column, second, time)


def slab_kernel(chunk, steps, tensor, second, time, total, turned, read, read_sem, ready, ready_sem, added):
    def fetch(step):
        source = tensor.at[:, pl.ds(step * chunk, chunk)]
        return pltpu.make_async_copy(source, read.at[step], read_sem.at[step])

    def put(step):
        target = turned.at[pl.ds(step * chunk, chunk)]
        return pltpu.make_async_copy(ready.at[step], target, ready_sem.at[step])

    for step in range(steps):
        fetch(step).start()
    time_wide = time[...].astype(jnp.float32)
    added[...] = jnp.zeros_like(added)

    def body(step, carry):
        fetch(step).wait()
        block = jnp.swapaxes(read[step], 0, 1)
        for j in range(chunk):
            ready[step, j] = block[j].T
        put(step).start()
        row = pl.multiple_of(step * chunk, chunk)
        weights = second[pl.ds(row, chunk), :].astype(jnp.float32)
        khatri = jnp.concatenate(
            [(weights[j : j + 1, :] * time_wide).astype(jnp.bfloat16) for j in range(chunk)], 0
        )
        tiles = jnp.concatenate([block[j] for j in range(chunk)], 1)
        added[...] += jnp.dot(tiles, khatri, preferred_element_type=jnp.float32)
        return carry

    lax.fori_loop(0, steps, body, 0)
    total[...] = added[...].T

    def finish(step, carry):
        put(step).wait()
        return carry

    lax.fori_loop(0, steps, finish, 0)


def slab_and_turn(tensor, second, time):
    tile_i, tile_j, tile_k = tensor.shape
    rank = time.shape[1]
    chunk = chunk_of(tile_j, 16)
    steps = tile_j // chunk
    return kernel_call(
        functools.partial(slab_kernel, chunk, steps),
        2 * tile_i * tile_j * tile_k * rank,
        4 * tile_i * tile_j * tile_k,
        out_shape=(
            jax.ShapeDtypeStruct((rank, tile_i), jnp.float32),
            pltpu.HBM((tile_j, tile_k, tile_i), tensor.dtype),
        ),
        in_specs=[ANY, VMEM, VMEM],
        out_specs=(VMEM, ANY),
        scratch_shapes=[
            pltpu.VMEM((steps, tile_i, chunk, tile_k), tensor.dtype),
            pltpu.SemaphoreType.DMA((steps,)),
            pltpu.VMEM((steps, chunk, tile_k, tile_i), tensor.dtype),
            pltpu.SemaphoreType.DMA((steps,)),
            pltpu.VMEM((tile_i, rank), jnp.float32),
        ],
    )(in_hbm(tensor), second, time)


def fetcher(turned, read, read_sem, chunk):
    def fetch(step):
        source = turned.at[pl.ds(step * chunk, chunk)]
        return pltpu.make_async_copy(source, read.at[step], read_sem.at[step])

    for step in range(read.shape[0]):
        fetch(step).start()
    return fetch


def plane_kernel(chunk, turned, first_turned, time, total, first, read, read_sem):
    fetch = fetcher(turned, read, read_sem, chunk)
    first[...] = first_turned[...].T
    shared = first[...]

    def body(step, carry):
        fetch(step).wait()
        sums = []
        for j in range(chunk):
            weighted = jnp.dot(read[step, j], shared, preferred_element_type=jnp.float32)
            scaled = weighted * time[...].astype(jnp.float32)
            sums.append(jnp.sum(scaled, axis=0, keepdims=True))
        row = pl.multiple_of(step * chunk, chunk)
        total[pl.ds(row, chunk), :] = jnp.concatenate(sums, 0)
        return carry

    lax.fori_loop(0, read.shape[0], body, 0)


def time_kernel(chunk, turned, first, second, total, read, read_sem, wide):
    fetch = fetcher(turned, read, read_sem, chunk)
    wide[...] = second[...].astype(jnp.float32)
    total[...] = jnp.zeros_like(total)
    shared = first[...]

    def body(step, carry):
        fetch(step).wait()
        part = total[...]
        for j in range(chunk):
            weighted = jnp.dot(read[step, j], shared, preferred_element_type=jnp.float32)
            part = part + weighted * wide[pl.ds(step * chunk + j, 1), :]
        total[...] = part
        return carry

    lax.fori_loop(0, read.shape[0], body, 0)


def weighted_call(kernel, turned, args, outs, extra=()):
    tile_j, tile_k, tile_i = turned.shape
    chunk = chunk_of(tile_j, 16)
    steps = tile_j // chunk
    rank = args[0].shape[0]
    return kernel_call(
        functools.partial(kernel, chunk),
        2 * tile_i * tile_j * tile_k * rank,
        2 * tile_i * tile_j * tile_k,
        out_shape=outs,
        in_specs=[ANY] + [VMEM] * len(args),
        out_specs=(VMEM,) * len(outs),
        scratch_shapes=[
            pltpu.VMEM((steps, chunk, tile_k, tile_i), turned.dtype),
            pltpu.SemaphoreType.DMA((steps,)),
            *extra,
        ],
    )(in_hbm(turned), *args)


def cross_product(values):
    return lax.dot_general(
        values, values, (((0,), (0,)), ((), ())), preferred_element_type=jnp.float32
    )


def row_product(values):
    return lax.dot_general(
        values, values, (((1,), (1,)), ((), ())), preferred_element_type=jnp.float32
    )


def swap(values, axis, size, mask):
    return lax.ppermute(values, axis, [(i, i ^ mask) for i in range(size)])


def halve(values, axis, size, mask, dim=0):
    half = values.shape[dim] // 2
    bit = (lax.axis_index(axis) & mask) // mask
    kept = lax.dynamic_slice_in_dim(values, bit * half, half, dim)
    sent = lax.dynamic_slice_in_dim(values, (1 - bit) * half, half, dim)
    return kept + swap(sent, axis, size, mask)


def double(values, axis, size, mask):
    other = swap(values, axis, size, mask)
    bit = (lax.axis_index(axis) & mask) // mask
    return jnp.where(
        bit == 0,
        jnp.concatenate([values, other], 0),
        jnp.concatenate([other, values], 0),
    )


def tree_sum(terms):
    while len(terms) > 1:
        terms = [terms[i] + terms[i + 1] for i in range(0, len(terms), 2)]
    return terms[0]


def masks_of(size):
    return [1 << b for b in range(size.bit_length() - 1)]


def spread(values, axis, size, step=1):
    return [values] + [swap(values, axis, size, d) for d in range(step, size, step)]


def all_sum(values, axis, size, step=1):
    return tree_sum(spread(values, axis, size, step))


def full_dot(left, right, dims):
    return lax.dot_general(
        left, right, (dims, ((), ())), precision=lax.Precision.HIGHEST,
        preferred_element_type=jnp.float32,
    )


def on_device(
    size_i, size_j, size_k, tensor, matrix, first_factor, second_factor, time_factor, column_factor
):
    f32 = jnp.float32
    tile_i, tile_j, tile_k = tensor.shape
    rank = first_factor.shape[1]
    share = rank // size_j
    part = 0
    for mask in masks_of(size_j):
        part = 2 * part + (lax.axis_index("ja") & mask) // mask

    coupled, grams, gram_time = local_products(matrix, column_factor, second_factor, time_factor)
    for mask in masks_of(size_j):
        grams = halve(grams, "ja", size_j, mask)
    gram_second = grams[:, rank:]
    time_rows = lax.dynamic_slice_in_dim(gram_time, part * share, share, 0)
    grams = jnp.concatenate([grams[:, :rank], time_rows], 1)
    for mask in masks_of(size_k):
        grams = grams + swap(grams, "ka", size_k, mask)
    gram_column, time_rows = grams[:, :rank], grams[:, rank:]
    gram_column = all_sum(gram_column, "ia", size_i)
    gram_total = gram_second * time_rows + gram_column
    first_wide = first_factor.astype(f32)
    denominator = full_dot(gram_total, first_wide, ((1,), (1,)))

    for mask in reversed(masks_of(size_i)):
        coupled = halve(coupled, "ia", size_i, mask, 1)
    slab, turned = slab_and_turn(tensor, second_factor, time_factor)
    numerator = slab + coupled
    for mask in masks_of(size_j):
        numerator = halve(numerator, "ja", size_j, mask)
    numerator = all_sum(numerator, "ka", size_k)
    own = lax.dynamic_slice_in_dim(first_wide.T, part * share, share, 0)
    first_new = (own * numerator / denominator).astype(jnp.bfloat16)
    for mask in reversed(masks_of(size_j)):
        first_new = double(first_new, "ja", size_j, mask)

    firsts = spread(first_new, "ia", size_i)
    gram_first = tree_sum([row_product(piece) for piece in firsts])
    times = time_factor
    for mask in masks_of(size_k):
        times = double(times, "ka", size_k, mask)
    gram_time = cross_product(times)
    plane_sum, first_out = weighted_call(
        plane_kernel,
        turned,
        (first_new, time_factor),
        (
            jax.ShapeDtypeStruct((tile_j, rank), f32),
            jax.ShapeDtypeStruct((tile_i, rank), jnp.bfloat16),
        ),
    )
    for mask in reversed(masks_of(size_i)):
        plane_sum = halve(plane_sum, "ia", size_i, mask)
    plane_sum = all_sum(plane_sum, "ka", size_k)
    rows = tile_j // size_i
    own = lax.dynamic_slice_in_dim(second_factor, lax.axis_index("ia") * rows, rows, 0).astype(f32)
    denominator = full_dot(own, gram_first * gram_time, ((1,), (0,)))
    second_new = (own * plane_sum / denominator).astype(jnp.bfloat16)
    for mask in masks_of(size_i):
        second_new = double(second_new, "ia", size_i, mask)

    seconds = second_new
    for mask in reversed(masks_of(size_j)):
        seconds = double(seconds, "ja", size_j, mask)
    gram_new = cross_product(seconds)
    (time_sum,) = weighted_call(
        time_kernel,
        turned,
        (first_out, second_new),
        (jax.ShapeDtypeStruct((tile_k, rank), f32),),
        (pltpu.VMEM((tile_j, rank), f32),),
    )
    time_sum = halve(time_sum, "ja", size_j, 1)
    time_sum = all_sum(time_sum, "ja", size_j, 2)
    time_sum = all_sum(time_sum, "ia", size_i)
    rows = tile_k // 2
    own = lax.dynamic_slice_in_dim(
        time_factor, (lax.axis_index("ja") % 2) * rows, rows, 0
    ).astype(f32)
    denominator = full_dot(own, gram_first * gram_new, ((1,), (0,)))
    time_new = (own * time_sum / denominator).astype(jnp.bfloat16)
    time_new = double(time_new, "ja", size_j, 1)
    return (first_out, second_new, time_new)


def in_layer(sizes, *args):
    return on_device(*sizes, *args)


def solution(mesh):
    sizes = (mesh.shape["ia"], mesh.shape["ja"], mesh.shape["ka"])
    return jax.shard_map(
        functools.partial(in_layer, sizes),
        mesh=mesh,
        in_specs=(
            P("ia", "ja", "ka"),
            P(None, ("ia", "ja", "ka")),
            P("ia", None),
            P("ja", None),
            P("ka", None),
            P(("ia", "ja", "ka"), None),
        ),
        out_specs=(P("ia", None), P("ja", None), P("ka", None)),
        check_vma=False,
    )
```

```python
import functools

import jax
import jax.numpy as jnp
from jax import lax
from jax.experimental import pallas as pl
from jax.experimental.pallas import tpu as pltpu
from jax.sharding import PartitionSpec as P


ANY = pl.BlockSpec(memory_space=pl.ANY)
VMEM = pl.BlockSpec(memory_space=pltpu.VMEM)
LIMIT = 32 << 20


def in_hbm(values):
    return pltpu.with_memory_space_constraint(values, pltpu.HBM)


def chunk_of(length, most):
    size = min(length, most)
    while length % size:
        size //= 2
    return size


def kernel_call(kernel, flops, nbytes, **kwargs):
    return pl.pallas_call(
        kernel,
        cost_estimate=pl.CostEstimate(flops=flops, bytes_accessed=nbytes, transcendentals=0),
        compiler_params=pltpu.CompilerParams(vmem_limit_bytes=LIMIT),
        **kwargs,
    )


def bring(sources, targets, sem):
    def copy(index):
        return pltpu.make_async_copy(sources[index], targets[index], sem.at[index])

    for index in range(len(sources)):
        copy(index).start()
    return lambda index: copy(index).wait()


def local_kernel(matrix, column, second, time, coupled, grams, gram_time, *scratch):
    f32 = jnp.float32
    *held, sem = scratch
    wait = bring((column, second, time, matrix), held, sem)
    rank = column.shape[1]
    held_column, held_second, held_time, held_matrix = held
    wait(0)
    turned = held_column[...].T
    grams[:, :rank] = jnp.dot(turned, held_column[...], preferred_element_type=f32)
    wait(1)
    grams[:, rank:] = jnp.dot(held_second[...].T, held_second[...], preferred_element_type=f32)
    wait(2)
    gram_time[...] = jnp.dot(held_time[...].T, held_time[...], preferred_element_type=f32)
    wait(3)
    coupled[...] = lax.dot_general(
        turned, held_matrix[...], (((1,), (1,)), ((), ())), preferred_element_type=f32
    )


def local_products(matrix, column, second, time):
    rank = column.shape[1]
    rows, width = matrix.shape
    f32 = jnp.float32
    return kernel_call(
        local_kernel,
        2 * width * rank * (rows + rank),
        2 * width * (rows + rank),
        out_shape=(
            jax.ShapeDtypeStruct((rank, rows), f32),
            jax.ShapeDtypeStruct((rank, 2 * rank), f32),
            jax.ShapeDtypeStruct((rank, rank), f32),
        ),
        in_specs=[ANY] * 4,
        out_specs=(VMEM,) * 3,
        scratch_shapes=[
            *(pltpu.VMEM(a.shape, a.dtype) for a in (column, second, time, matrix)),
            pltpu.SemaphoreType.DMA((4,)),
        ],
    )(*(in_hbm(a) for a in (matrix, column, second, time)))


def slab_kernel(chunk, steps, tensor, second_in, time_in, total, turned, *scratch):
    read, read_sem, ready, ready_sem, added, second, time, sem = scratch
    wait = bring((second_in, time_in), (second, time), sem)

    def fetch(step):
        source = tensor.at[:, pl.ds(step * chunk, chunk)]
        return pltpu.make_async_copy(source, read.at[step], read_sem.at[step])

    def put(step):
        target = turned.at[pl.ds(step * chunk, chunk)]
        return pltpu.make_async_copy(ready.at[step], target, ready_sem.at[step])

    for step in range(steps):
        fetch(step).start()
    wait(0)
    wait(1)
    time_wide = time[...].astype(jnp.float32)
    added[...] = jnp.zeros_like(added)

    def body(step, carry):
        fetch(step).wait()
        block = jnp.swapaxes(read[step], 0, 1)
        for j in range(chunk):
            ready[step, j] = block[j].T
        put(step).start()
        row = pl.multiple_of(step * chunk, chunk)
        weights = second[pl.ds(row, chunk), :].astype(jnp.float32)
        khatri = jnp.concatenate(
            [(weights[j : j + 1, :] * time_wide).astype(jnp.bfloat16) for j in range(chunk)], 0
        )
        tiles = jnp.concatenate([block[j] for j in range(chunk)], 1)
        added[...] += jnp.dot(tiles, khatri, preferred_element_type=jnp.float32)
        return carry

    lax.fori_loop(0, steps, body, 0)
    total[...] = added[...].T

    def finish(step, carry):
        put(step).wait()
        return carry

    lax.fori_loop(0, steps, finish, 0)


def slab_and_turn(tensor, second, time):
    tile_i, tile_j, tile_k = tensor.shape
    rank = time.shape[1]
    chunk = chunk_of(tile_j, 16)
    steps = tile_j // chunk
    return kernel_call(
        functools.partial(slab_kernel, chunk, steps),
        2 * tile_i * tile_j * tile_k * rank,
        4 * tile_i * tile_j * tile_k,
        out_shape=(
            jax.ShapeDtypeStruct((rank, tile_i), jnp.float32),
            pltpu.HBM((tile_j, tile_k, tile_i), tensor.dtype),
        ),
        in_specs=[ANY] * 3,
        out_specs=(VMEM, ANY),
        scratch_shapes=[
            pltpu.VMEM((steps, tile_i, chunk, tile_k), tensor.dtype),
            pltpu.SemaphoreType.DMA((steps,)),
            pltpu.VMEM((steps, chunk, tile_k, tile_i), tensor.dtype),
            pltpu.SemaphoreType.DMA((steps,)),
            pltpu.VMEM((tile_i, rank), jnp.float32),
            pltpu.VMEM(second.shape, second.dtype),
            pltpu.VMEM(time.shape, time.dtype),
            pltpu.SemaphoreType.DMA((2,)),
        ],
    )(in_hbm(tensor), in_hbm(second), in_hbm(time))


def fetcher(turned, read, read_sem, chunk):
    def fetch(step):
        source = turned.at[pl.ds(step * chunk, chunk)]
        return pltpu.make_async_copy(source, read.at[step], read_sem.at[step])

    for step in range(read.shape[0]):
        fetch(step).start()
    return fetch


def plane_kernel(chunk, turned, first_turned, time, total, first, read, read_sem):
    fetch = fetcher(turned, read, read_sem, chunk)
    first[...] = first_turned[...].T
    shared = first[...]

    def body(step, carry):
        fetch(step).wait()
        sums = []
        for j in range(chunk):
            weighted = jnp.dot(read[step, j], shared, preferred_element_type=jnp.float32)
            scaled = weighted * time[...].astype(jnp.float32)
            sums.append(jnp.sum(scaled, axis=0, keepdims=True))
        row = pl.multiple_of(step * chunk, chunk)
        total[pl.ds(row, chunk), :] = jnp.concatenate(sums, 0)
        return carry

    lax.fori_loop(0, read.shape[0], body, 0)


def time_kernel(chunk, turned, first_in, second, total, read, read_sem, wide, first, sem):
    wait = bring((first_in,), (first,), sem)
    fetch = fetcher(turned, read, read_sem, chunk)
    wide[...] = second[...].astype(jnp.float32)
    total[...] = jnp.zeros_like(total)
    wait(0)
    shared = first[...]

    def body(step, carry):
        fetch(step).wait()
        part = total[...]
        for j in range(chunk):
            weighted = jnp.dot(read[step, j], shared, preferred_element_type=jnp.float32)
            part = part + weighted * wide[pl.ds(step * chunk + j, 1), :]
        total[...] = part
        return carry

    lax.fori_loop(0, read.shape[0], body, 0)


def weighted_call(kernel, turned, args, specs, outs, extra=()):
    tile_j, tile_k, tile_i = turned.shape
    chunk = chunk_of(tile_j, 16)
    steps = tile_j // chunk
    rank = args[0].shape[0]
    return kernel_call(
        functools.partial(kernel, chunk),
        2 * tile_i * tile_j * tile_k * rank,
        2 * tile_i * tile_j * tile_k,
        out_shape=outs,
        in_specs=[ANY, *specs],
        out_specs=(VMEM,) * len(outs),
        scratch_shapes=[
            pltpu.VMEM((steps, chunk, tile_k, tile_i), turned.dtype),
            pltpu.SemaphoreType.DMA((steps,)),
            *extra,
        ],
    )(in_hbm(turned), *args)


def cross_product(values):
    return lax.dot_general(
        values, values, (((0,), (0,)), ((), ())), preferred_element_type=jnp.float32
    )


def row_product(values):
    return lax.dot_general(
        values, values, (((1,), (1,)), ((), ())), preferred_element_type=jnp.float32
    )


def swap(values, axis, size, mask):
    return lax.ppermute(values, axis, [(i, i ^ mask) for i in range(size)])


def halve(values, axis, size, mask, dim=0):
    half = values.shape[dim] // 2
    bit = (lax.axis_index(axis) & mask) // mask
    kept = lax.dynamic_slice_in_dim(values, bit * half, half, dim)
    sent = lax.dynamic_slice_in_dim(values, (1 - bit) * half, half, dim)
    return kept + swap(sent, axis, size, mask)


def in_order(own, other, axis, mask):
    bit = (lax.axis_index(axis) & mask) // mask
    return jnp.where(
        bit == 0, jnp.concatenate([own, other], 0), jnp.concatenate([other, own], 0)
    )


def double(values, axis, size, mask):
    return in_order(values, swap(values, axis, size, mask), axis, mask)


def tree_sum(terms):
    while len(terms) > 1:
        terms = [terms[i] + terms[i + 1] for i in range(0, len(terms), 2)]
    return terms[0]


def masks_of(size):
    return [1 << b for b in range(size.bit_length() - 1)]


def spread(values, axis, size, step=1):
    return [values] + [swap(values, axis, size, d) for d in range(step, size, step)]


def all_sum(values, axis, size, step=1):
    return tree_sum(spread(values, axis, size, step))


def full_dot(left, right, dims):
    return lax.dot_general(
        left, right, (dims, ((), ())), precision=lax.Precision.HIGHEST,
        preferred_element_type=jnp.float32,
    )


def on_device(
    size_i, size_j, size_k, tensor, matrix, first_factor, second_factor, time_factor, column_factor
):
    f32 = jnp.float32
    tile_i, tile_j, tile_k = tensor.shape
    rank = first_factor.shape[1]
    share = rank // size_j
    part = 0
    for mask in masks_of(size_j):
        part = 2 * part + (lax.axis_index("ja") & mask) // mask

    coupled, grams, gram_time = local_products(matrix, column_factor, second_factor, time_factor)
    for mask in masks_of(size_j):
        grams = halve(grams, "ja", size_j, mask)
    gram_second = grams[:, rank:]
    time_rows = lax.dynamic_slice_in_dim(gram_time, part * share, share, 0)
    grams = jnp.concatenate([grams[:, :rank], time_rows], 1)
    times = time_factor
    for mask in masks_of(size_k):
        if mask == 1:
            wide = jnp.concatenate([times[: tile_k // 2], times[tile_k // 2 :]], 1)
            sent = jnp.concatenate([grams, wide.astype(f32)], 0)
            came = swap(sent, "ka", size_k, mask)
            grams = grams + came[:share]
            other = came[share:].astype(jnp.bfloat16)
            other = jnp.concatenate([other[:, :rank], other[:, rank:]], 0)
            times = in_order(times, other, "ka", mask)
        else:
            grams = grams + swap(grams, "ka", size_k, mask)
    gram_column, time_rows = grams[:, :rank], grams[:, rank:]
    gram_column = all_sum(gram_column, "ia", size_i)
    gram_total = gram_second * time_rows + gram_column
    first_wide = first_factor.astype(f32)
    denominator = full_dot(gram_total, first_wide, ((1,), (1,)))

    for mask in reversed(masks_of(size_i)):
        coupled = halve(coupled, "ia", size_i, mask, 1)
    slab, turned = slab_and_turn(tensor, second_factor, time_factor)
    numerator = slab + coupled
    for mask in masks_of(size_j):
        numerator = halve(numerator, "ja", size_j, mask)
    numerator = all_sum(numerator, "ka", size_k)
    own = lax.dynamic_slice_in_dim(first_wide.T, part * share, share, 0)
    first_new = (own * numerator / denominator).astype(jnp.bfloat16)
    for mask in reversed(masks_of(size_j)):
        first_new = double(first_new, "ja", size_j, mask)

    firsts = spread(first_new, "ia", size_i)
    gram_first = tree_sum([row_product(piece) for piece in firsts])
    for mask in masks_of(size_k)[1:]:
        times = double(times, "ka", size_k, mask)
    gram_time = cross_product(times)
    plane_sum, first_out = weighted_call(
        plane_kernel,
        turned,
        (first_new, time_factor),
        (VMEM, VMEM),
        (
            jax.ShapeDtypeStruct((tile_j, rank), f32),
            jax.ShapeDtypeStruct((tile_i, rank), jnp.bfloat16),
        ),
    )
    for mask in reversed(masks_of(size_i)):
        plane_sum = halve(plane_sum, "ia", size_i, mask)
    plane_sum = all_sum(plane_sum, "ka", size_k)
    rows = tile_j // size_i
    own = lax.dynamic_slice_in_dim(second_factor, lax.axis_index("ia") * rows, rows, 0).astype(f32)
    denominator = full_dot(own, gram_first * gram_time, ((1,), (0,)))
    second_new = (own * plane_sum / denominator).astype(jnp.bfloat16)
    for mask in masks_of(size_i):
        second_new = double(second_new, "ia", size_i, mask)

    seconds = second_new
    for mask in reversed(masks_of(size_j)):
        seconds = double(seconds, "ja", size_j, mask)
    gram_new = cross_product(seconds)
    (time_sum,) = weighted_call(
        time_kernel,
        turned,
        (in_hbm(first_out), second_new),
        (ANY, VMEM),
        (jax.ShapeDtypeStruct((tile_k, rank), f32),),
        (
            pltpu.VMEM((tile_j, rank), f32),
            pltpu.VMEM((tile_i, rank), jnp.bfloat16),
            pltpu.SemaphoreType.DMA((1,)),
        ),
    )
    time_sum = halve(time_sum, "ja", size_j, 1)
    time_sum = all_sum(time_sum, ("ia", "ja"), size_i * size_j, 2)
    rows = tile_k // 2
    own = lax.dynamic_slice_in_dim(
        time_factor, (lax.axis_index("ja") % 2) * rows, rows, 0
    ).astype(f32)
    denominator = full_dot(own, gram_first * gram_new, ((1,), (0,)))
    time_new = (own * time_sum / denominator).astype(jnp.bfloat16)
    time_new = double(time_new, "ja", size_j, 1)
    return (first_out, second_new, time_new)


def in_layer(sizes, *args):
    return on_device(*sizes, *args)


def solution(mesh):
    sizes = (mesh.shape["ia"], mesh.shape["ja"], mesh.shape["ka"])
    return jax.shard_map(
        functools.partial(in_layer, sizes),
        mesh=mesh,
        in_specs=(
            P("ia", "ja", "ka"),
            P(None, ("ia", "ja", "ka")),
            P("ia", None),
            P("ja", None),
            P("ka", None),
            P(("ia", "ja", "ka"), None),
        ),
        out_specs=(P("ia", None), P("ja", None), P("ka", None)),
        check_vma=False,
    )
```

```python
import functools

import jax
import jax.numpy as jnp
from jax import lax
from jax.experimental import pallas as pl
from jax.experimental.pallas import tpu as pltpu
from jax.sharding import PartitionSpec as P


ANY = pl.BlockSpec(memory_space=pl.ANY)
VMEM = pl.BlockSpec(memory_space=pltpu.VMEM)
LIMIT = 32 << 20


def in_hbm(values):
    return pltpu.with_memory_space_constraint(values, pltpu.HBM)


def chunk_of(length, most):
    size = min(length, most)
    while length % size:
        size //= 2
    return size


def kernel_call(kernel, flops, nbytes, **kwargs):
    return pl.pallas_call(
        kernel,
        cost_estimate=pl.CostEstimate(flops=flops, bytes_accessed=nbytes, transcendentals=0),
        compiler_params=pltpu.CompilerParams(vmem_limit_bytes=LIMIT),
        **kwargs,
    )


def bring(sources, targets, sem):
    def copy(index):
        return pltpu.make_async_copy(sources[index], targets[index], sem.at[index])

    for index in range(len(sources)):
        copy(index).start()
    return lambda index: copy(index).wait()


def gram_kernel(column, second, time, grams, gram_time, turned, second_out, time_out, held, sem):
    f32 = jnp.float32
    wait = bring((column, second, time), (held, second_out, time_out), sem)
    rank = column.shape[1]
    wait(0)
    turned[...] = held[...].T
    grams[:, :rank] = jnp.dot(turned[...], held[...], preferred_element_type=f32)
    wait(1)
    grams[:, rank:] = jnp.dot(second_out[...].T, second_out[...], preferred_element_type=f32)
    wait(2)
    gram_time[...] = jnp.dot(time_out[...].T, time_out[...], preferred_element_type=f32)


def local_grams(column, second, time):
    width, rank = column.shape
    f32 = jnp.float32
    return kernel_call(
        gram_kernel,
        2 * width * rank * rank,
        2 * width * rank,
        out_shape=(
            jax.ShapeDtypeStruct((rank, 2 * rank), f32),
            jax.ShapeDtypeStruct((rank, rank), f32),
            jax.ShapeDtypeStruct((rank, width), column.dtype),
            jax.ShapeDtypeStruct(second.shape, second.dtype),
            jax.ShapeDtypeStruct(time.shape, time.dtype),
        ),
        in_specs=[ANY] * 3,
        out_specs=(VMEM,) * 5,
        scratch_shapes=[
            pltpu.VMEM(column.shape, column.dtype),
            pltpu.SemaphoreType.DMA((3,)),
        ],
    )(*(in_hbm(a) for a in (column, second, time)))


def coupled_kernel(turned, matrix, coupled):
    coupled[...] = lax.dot_general(
        turned[...], matrix[...], (((1,), (1,)), ((), ())), preferred_element_type=jnp.float32
    )


def local_coupled(turned, matrix):
    rank, width = turned.shape
    rows = matrix.shape[0]
    return kernel_call(
        coupled_kernel,
        2 * width * rank * rows,
        2 * width * (rows + rank),
        out_shape=jax.ShapeDtypeStruct((rank, rows), jnp.float32),
        in_specs=[VMEM] * 2,
        out_specs=VMEM,
    )(turned, matrix)


def slab_kernel(first, chunk, steps, tensor, second, time, *refs):
    *start, total, turned, read, read_sem, ready, ready_sem, added = refs
    ahead = min(3, steps)

    def fetch(step):
        source = tensor.at[:, pl.ds(first + step * chunk, chunk)]
        return pltpu.make_async_copy(source, read.at[step], read_sem.at[step])

    def put(step):
        target = turned.at[pl.ds(step * chunk, chunk)]
        return pltpu.make_async_copy(ready.at[step], target, ready_sem.at[step])

    for step in range(ahead):
        fetch(step).start()
    time_wide = time[...].astype(jnp.float32)
    added[...] = start[0][...] if start else jnp.zeros_like(added)

    def body(step, carry):
        fetch(step).wait()

        @pl.when(step + ahead < steps)
        def _():
            fetch(step + ahead).start()

        block = jnp.swapaxes(read[step], 0, 1)
        for j in range(chunk):
            ready[step, j] = block[j].T
        put(step).start()
        row = pl.multiple_of(first + step * chunk, chunk)
        weights = second[pl.ds(row, chunk), :].astype(jnp.float32)
        khatri = jnp.concatenate(
            [(weights[j : j + 1, :] * time_wide).astype(jnp.bfloat16) for j in range(chunk)], 0
        )
        tiles = jnp.concatenate([block[j] for j in range(chunk)], 1)
        added[...] += jnp.dot(tiles, khatri, preferred_element_type=jnp.float32)
        return carry

    lax.fori_loop(0, steps, body, 0)
    total[...] = added[...].T if start else added[...]

    def finish(step, carry):
        put(step).wait()
        return carry

    lax.fori_loop(0, steps, finish, 0)


def slab_and_turn(tensor, second, time, first, count, start=()):
    tile_i, _, tile_k = tensor.shape
    rank = time.shape[1]
    chunk = chunk_of(count, 8)
    steps = count // chunk
    return kernel_call(
        functools.partial(slab_kernel, first, chunk, steps),
        2 * tile_i * count * tile_k * rank,
        4 * tile_i * count * tile_k,
        out_shape=(
            jax.ShapeDtypeStruct((rank, tile_i) if start else (tile_i, rank), jnp.float32),
            pltpu.HBM((count, tile_k, tile_i), tensor.dtype),
        ),
        in_specs=[ANY] + [VMEM] * (2 + len(start)),
        out_specs=(VMEM, ANY),
        scratch_shapes=[
            pltpu.VMEM((steps, tile_i, chunk, tile_k), tensor.dtype),
            pltpu.SemaphoreType.DMA((steps,)),
            pltpu.VMEM((steps, chunk, tile_k, tile_i), tensor.dtype),
            pltpu.SemaphoreType.DMA((steps,)),
            pltpu.VMEM((tile_i, rank), jnp.float32),
        ],
    )(in_hbm(tensor), second, time, *start)


def fetcher(parts, read, read_sem, chunk):
    steps = parts[0].shape[0] // chunk

    def fetch(part, step):
        source = parts[part].at[pl.ds(step * chunk, chunk)]
        slot = part * steps + step
        return pltpu.make_async_copy(source, read.at[slot], read_sem.at[slot])

    for part in range(len(parts)):
        for step in range(steps):
            fetch(part, step).start()
    return fetch, steps


def plane_kernel(chunk, parts, first_turned, time, total, first, read, read_sem):
    fetch, steps = fetcher(parts, read, read_sem, chunk)
    first[...] = first_turned[...].T
    shared = first[...]
    for part in range(len(parts)):

        def body(step, carry):
            fetch(part, step).wait()
            slot = part * steps + step
            sums = []
            for j in range(chunk):
                weighted = jnp.dot(read[slot, j], shared, preferred_element_type=jnp.float32)
                scaled = weighted * time[...].astype(jnp.float32)
                sums.append(jnp.sum(scaled, axis=0, keepdims=True))
            row = pl.multiple_of(slot * chunk, chunk)
            total[pl.ds(row, chunk), :] = jnp.concatenate(sums, 0)
            return carry

        lax.fori_loop(0, steps, body, 0)


def time_kernel(chunk, parts, first_turned, second, total, read, read_sem, wide, first):
    fetch, steps = fetcher(parts, read, read_sem, chunk)
    wide[...] = second[...].astype(jnp.float32)
    first[...] = first_turned[...].T
    total[...] = jnp.zeros_like(total)
    shared = first[...]
    for part in range(len(parts)):

        def body(step, carry):
            fetch(part, step).wait()
            slot = part * steps + step
            sums = total[...]
            for j in range(chunk):
                weighted = jnp.dot(read[slot, j], shared, preferred_element_type=jnp.float32)
                sums = sums + weighted * wide[pl.ds(slot * chunk + j, 1), :]
            total[...] = sums
            return carry

        lax.fori_loop(0, steps, body, 0)


def weighted_call(kernel, parts, args, outs, extra=()):
    count, tile_k, tile_i = parts[0].shape
    chunk = chunk_of(count, 16)
    slots = len(parts) * count // chunk
    rank = args[0].shape[0]

    def on_parts(*refs):
        kernel(chunk, refs[: len(parts)], *refs[len(parts) :])

    return kernel_call(
        on_parts,
        2 * tile_i * len(parts) * count * tile_k * rank,
        2 * tile_i * len(parts) * count * tile_k,
        out_shape=outs,
        in_specs=[ANY] * len(parts) + [VMEM] * len(args),
        out_specs=(VMEM,) * len(outs),
        scratch_shapes=[
            pltpu.VMEM((slots, chunk, tile_k, tile_i), parts[0].dtype),
            pltpu.SemaphoreType.DMA((slots,)),
            *extra,
        ],
    )(*(in_hbm(a) for a in parts), *args)


def cross_product(values):
    return lax.dot_general(
        values, values, (((0,), (0,)), ((), ())), preferred_element_type=jnp.float32
    )


def row_product(values):
    return lax.dot_general(
        values, values, (((1,), (1,)), ((), ())), preferred_element_type=jnp.float32
    )


def swap(values, axis, size, mask):
    return lax.ppermute(values, axis, [(i, i ^ mask) for i in range(size)])


def halve(values, axis, size, mask, dim=0):
    half = values.shape[dim] // 2
    bit = (lax.axis_index(axis) & mask) // mask
    kept = lax.dynamic_slice_in_dim(values, bit * half, half, dim)
    sent = lax.dynamic_slice_in_dim(values, (1 - bit) * half, half, dim)
    return kept + swap(sent, axis, size, mask)


def in_order(own, other, axis, mask):
    bit = (lax.axis_index(axis) & mask) // mask
    return jnp.where(
        bit == 0, jnp.concatenate([own, other], 0), jnp.concatenate([other, own], 0)
    )


def double(values, axis, size, mask):
    return in_order(values, swap(values, axis, size, mask), axis, mask)


def tree_sum(terms):
    while len(terms) > 1:
        terms = [terms[i] + terms[i + 1] for i in range(0, len(terms), 2)]
    return terms[0]


def masks_of(size):
    return [1 << b for b in range(size.bit_length() - 1)]


def spread(values, axis, size, step=1):
    return [values] + [swap(values, axis, size, d) for d in range(step, size, step)]


def all_sum(values, axis, size, step=1):
    return tree_sum(spread(values, axis, size, step))


def full_dot(left, right, dims):
    return lax.dot_general(
        left, right, (dims, ((), ())), precision=lax.Precision.HIGHEST,
        preferred_element_type=jnp.float32,
    )


def on_device(
    size_i, size_j, size_k, tensor, matrix, first_factor, second_factor, time_factor, column_factor
):
    f32 = jnp.float32
    tile_i, tile_j, tile_k = tensor.shape
    rank = first_factor.shape[1]
    share = rank // size_j
    part = 0
    for mask in masks_of(size_j):
        part = 2 * part + (lax.axis_index("ja") & mask) // mask

    grams, gram_time, column_turned, second_near, time_near = local_grams(
        column_factor, second_factor, time_factor
    )
    for mask in masks_of(size_j):
        grams = halve(grams, "ja", size_j, mask)
    gram_second = grams[:, rank:]
    time_rows = lax.dynamic_slice_in_dim(gram_time, part * share, share, 0)
    grams = jnp.concatenate([grams[:, :rank], time_rows], 1)
    grams = all_sum(grams, "ka", size_k)
    gram_column, time_rows = grams[:, :rank], grams[:, rank:]
    gram_column = all_sum(gram_column, "ia", size_i)
    gram_total = gram_second * time_rows + gram_column
    first_wide = first_factor.astype(f32)
    denominator = full_dot(gram_total, first_wide, ((1,), (1,)))

    coupled = local_coupled(column_turned, matrix)
    for mask in reversed(masks_of(size_i)):
        coupled = halve(coupled, "ia", size_i, mask, 1)
    half = tile_j // 2
    slab, low = slab_and_turn(tensor, second_near, time_near, 0, half)
    slab, high = slab_and_turn(tensor, second_near, time_near, half, half, (slab,))
    turned = (low, high)
    numerator = slab + coupled
    for mask in masks_of(size_j):
        numerator = halve(numerator, "ja", size_j, mask)
    numerator = all_sum(numerator, "ka", size_k)
    own = lax.dynamic_slice_in_dim(first_wide.T, part * share, share, 0)
    first_new = (own * numerator / denominator).astype(jnp.bfloat16)
    for mask in reversed(masks_of(size_j)):
        first_new = double(first_new, "ja", size_j, mask)

    firsts = spread(first_new, "ia", size_i)
    gram_first = tree_sum([row_product(piece) for piece in firsts])
    times = time_factor
    for mask in masks_of(size_k):
        times = double(times, "ka", size_k, mask)
    gram_time = cross_product(times)
    plane_sum, first_out = weighted_call(
        plane_kernel,
        turned,
        (first_new, time_factor),
        (
            jax.ShapeDtypeStruct((tile_j, rank), f32),
            jax.ShapeDtypeStruct((tile_i, rank), jnp.bfloat16),
        ),
    )
    for mask in reversed(masks_of(size_i)):
        plane_sum = halve(plane_sum, "ia", size_i, mask)
    plane_sum = all_sum(plane_sum, "ka", size_k)
    rows = tile_j // size_i
    own = lax.dynamic_slice_in_dim(second_factor, lax.axis_index("ia") * rows, rows, 0).astype(f32)
    denominator = full_dot(own, gram_first * gram_time, ((1,), (0,)))
    second_new = (own * plane_sum / denominator).astype(jnp.bfloat16)
    for mask in masks_of(size_i):
        second_new = double(second_new, "ia", size_i, mask)

    seconds = second_new
    for mask in reversed(masks_of(size_j)):
        seconds = double(seconds, "ja", size_j, mask)
    gram_new = cross_product(seconds)
    (time_sum,) = weighted_call(
        time_kernel,
        turned,
        (first_new, second_new),
        (jax.ShapeDtypeStruct((tile_k, rank), f32),),
        (
            pltpu.VMEM((tile_j, rank), f32),
            pltpu.VMEM((tile_i, rank), jnp.bfloat16),
        ),
    )
    time_sum = halve(time_sum, "ja", size_j, 1)
    time_sum = all_sum(time_sum, ("ia", "ja"), size_i * size_j, 2)
    rows = tile_k // 2
    own = lax.dynamic_slice_in_dim(
        time_factor, (lax.axis_index("ja") % 2) * rows, rows, 0
    ).astype(f32)
    denominator = full_dot(own, gram_first * gram_new, ((1,), (0,)))
    time_new = (own * time_sum / denominator).astype(jnp.bfloat16)
    time_new = double(time_new, "ja", size_j, 1)
    return (first_out, second_new, time_new)


def in_layer(sizes, *args):
    return on_device(*sizes, *args)


def solution(mesh):
    sizes = (mesh.shape["ia"], mesh.shape["ja"], mesh.shape["ka"])
    return jax.shard_map(
        functools.partial(in_layer, sizes),
        mesh=mesh,
        in_specs=(
            P("ia", "ja", "ka"),
            P(None, ("ia", "ja", "ka")),
            P("ia", None),
            P("ja", None),
            P("ka", None),
            P(("ia", "ja", "ka"), None),
        ),
        out_specs=(P("ia", None), P("ja", None), P("ka", None)),
        check_vma=False,
    )
```

```python
import functools

import jax
import jax.numpy as jnp
from jax import lax
from jax.experimental import pallas as pl
from jax.experimental.pallas import tpu as pltpu
from jax.sharding import PartitionSpec as P


ANY = pl.BlockSpec(memory_space=pl.ANY)
VMEM = pl.BlockSpec(memory_space=pltpu.VMEM)
LIMIT = 32 << 20


def in_hbm(values):
    return pltpu.with_memory_space_constraint(values, pltpu.HBM)


def chunk_of(length, most):
    size = min(length, most)
    while length % size:
        size //= 2
    return size


def kernel_call(kernel, flops, nbytes, **kwargs):
    return pl.pallas_call(
        kernel,
        cost_estimate=pl.CostEstimate(flops=flops, bytes_accessed=nbytes, transcendentals=0),
        compiler_params=pltpu.CompilerParams(vmem_limit_bytes=LIMIT),
        **kwargs,
    )


def bring(sources, targets, sem):
    def copy(index):
        return pltpu.make_async_copy(sources[index], targets[index], sem.at[index])

    for index in range(len(sources)):
        copy(index).start()
    return lambda index: copy(index).wait()


def local_kernel(
    column, second, time, matrix, grams, gram_time, coupled, second_out, time_out, *scratch
):
    f32 = jnp.float32
    held, held_matrix, turned, sem = scratch
    targets = (held, second_out, time_out, held_matrix)
    wait = bring((column, second, time, matrix), targets, sem)
    rank = column.shape[1]
    wait(0)
    turned[...] = held[...].T
    grams[:, :rank] = jnp.dot(turned[...], held[...], preferred_element_type=f32)
    wait(1)
    grams[:, rank:] = jnp.dot(second_out[...].T, second_out[...], preferred_element_type=f32)
    wait(2)
    gram_time[...] = jnp.dot(time_out[...].T, time_out[...], preferred_element_type=f32)
    wait(3)
    coupled[...] = lax.dot_general(
        turned[...], held_matrix[...], (((1,), (1,)), ((), ())), preferred_element_type=f32
    )


def local_products(column, second, time, matrix):
    width, rank = column.shape
    rows = matrix.shape[0]
    f32 = jnp.float32
    return kernel_call(
        local_kernel,
        2 * width * rank * (rank + rows),
        2 * width * (rank + rows),
        out_shape=(
            jax.ShapeDtypeStruct((rank, 2 * rank), f32),
            jax.ShapeDtypeStruct((rank, rank), f32),
            jax.ShapeDtypeStruct((rank, rows), f32),
            jax.ShapeDtypeStruct(second.shape, second.dtype),
            jax.ShapeDtypeStruct(time.shape, time.dtype),
        ),
        in_specs=[ANY] * 4,
        out_specs=(VMEM,) * 5,
        scratch_shapes=[
            pltpu.VMEM(column.shape, column.dtype),
            pltpu.VMEM(matrix.shape, matrix.dtype),
            pltpu.VMEM((rank, width), column.dtype),
            pltpu.SemaphoreType.DMA((4,)),
        ],
    )(*(in_hbm(a) for a in (column, second, time, matrix)))


def slab_kernel(first, chunk, steps, tensor, second, time, *refs):
    *start, total, turned, read, read_sem, ready, ready_sem, added = refs
    ahead = min(3, steps)

    def fetch(step):
        source = tensor.at[:, pl.ds(first + step * chunk, chunk)]
        return pltpu.make_async_copy(source, read.at[step], read_sem.at[step])

    def put(step):
        target = turned.at[pl.ds(step * chunk, chunk)]
        return pltpu.make_async_copy(ready.at[step], target, ready_sem.at[step])

    for step in range(ahead):
        fetch(step).start()
    time_wide = time[...].astype(jnp.float32)
    added[...] = start[0][...] if start else jnp.zeros_like(added)

    def body(step, carry):
        fetch(step).wait()

        @pl.when(step + ahead < steps)
        def _():
            fetch(step + ahead).start()

        block = jnp.swapaxes(read[step], 0, 1)
        for j in range(chunk):
            ready[step, j] = block[j].T
        put(step).start()
        row = pl.multiple_of(first + step * chunk, chunk)
        weights = second[pl.ds(row, chunk), :].astype(jnp.float32)
        khatri = jnp.concatenate(
            [(weights[j : j + 1, :] * time_wide).astype(jnp.bfloat16) for j in range(chunk)], 0
        )
        tiles = jnp.concatenate([block[j] for j in range(chunk)], 1)
        added[...] += jnp.dot(tiles, khatri, preferred_element_type=jnp.float32)
        return carry

    lax.fori_loop(0, steps, body, 0)
    total[...] = added[...].T if start else added[...]

    def finish(step, carry):
        put(step).wait()
        return carry

    lax.fori_loop(0, steps, finish, 0)


def slab_and_turn(tensor, second, time, first, count, start=()):
    tile_i, _, tile_k = tensor.shape
    rank = time.shape[1]
    chunk = chunk_of(count, 8)
    steps = count // chunk
    return kernel_call(
        functools.partial(slab_kernel, first, chunk, steps),
        2 * tile_i * count * tile_k * rank,
        4 * tile_i * count * tile_k,
        out_shape=(
            jax.ShapeDtypeStruct((rank, tile_i) if start else (tile_i, rank), jnp.float32),
            pltpu.HBM((count, tile_k, tile_i), tensor.dtype),
        ),
        in_specs=[ANY] + [VMEM] * (2 + len(start)),
        out_specs=(VMEM, ANY),
        scratch_shapes=[
            pltpu.VMEM((steps, tile_i, chunk, tile_k), tensor.dtype),
            pltpu.SemaphoreType.DMA((steps,)),
            pltpu.VMEM((steps, chunk, tile_k, tile_i), tensor.dtype),
            pltpu.SemaphoreType.DMA((steps,)),
            pltpu.VMEM((tile_i, rank), jnp.float32),
        ],
    )(in_hbm(tensor), second, time, *start)


def fetcher(parts, read, read_sem, chunk):
    steps = parts[0].shape[0] // chunk

    def fetch(part, step):
        source = parts[part].at[pl.ds(step * chunk, chunk)]
        slot = part * steps + step
        return pltpu.make_async_copy(source, read.at[slot], read_sem.at[slot])

    for part in range(len(parts)):
        for step in range(steps):
            fetch(part, step).start()
    return fetch, steps


def plane_kernel(chunk, parts, first_turned, time, total, first, read, read_sem):
    fetch, steps = fetcher(parts, read, read_sem, chunk)
    first[...] = first_turned[...].T
    shared = first[...]
    for part in range(len(parts)):

        def body(step, carry):
            fetch(part, step).wait()
            slot = part * steps + step
            sums = []
            for j in range(chunk):
                weighted = jnp.dot(read[slot, j], shared, preferred_element_type=jnp.float32)
                scaled = weighted * time[...].astype(jnp.float32)
                sums.append(jnp.sum(scaled, axis=0, keepdims=True))
            row = pl.multiple_of(slot * chunk, chunk)
            total[pl.ds(row, chunk), :] = jnp.concatenate(sums, 0)
            return carry

        lax.fori_loop(0, steps, body, 0)


def time_kernel(chunk, parts, first_turned, second, total, read, read_sem, wide, first):
    fetch, steps = fetcher(parts, read, read_sem, chunk)
    wide[...] = second[...].astype(jnp.float32)
    first[...] = first_turned[...].T
    total[...] = jnp.zeros_like(total)
    shared = first[...]
    for part in range(len(parts)):

        def body(step, carry):
            fetch(part, step).wait()
            slot = part * steps + step
            sums = total[...]
            for j in range(chunk):
                weighted = jnp.dot(read[slot, j], shared, preferred_element_type=jnp.float32)
                sums = sums + weighted * wide[pl.ds(slot * chunk + j, 1), :]
            total[...] = sums
            return carry

        lax.fori_loop(0, steps, body, 0)


def weighted_call(kernel, parts, args, outs, extra=()):
    count, tile_k, tile_i = parts[0].shape
    chunk = chunk_of(count, 16)
    slots = len(parts) * count // chunk
    rank = args[0].shape[0]

    def on_parts(*refs):
        kernel(chunk, refs[: len(parts)], *refs[len(parts) :])

    return kernel_call(
        on_parts,
        2 * tile_i * len(parts) * count * tile_k * rank,
        2 * tile_i * len(parts) * count * tile_k,
        out_shape=outs,
        in_specs=[ANY] * len(parts) + [VMEM] * len(args),
        out_specs=(VMEM,) * len(outs),
        scratch_shapes=[
            pltpu.VMEM((slots, chunk, tile_k, tile_i), parts[0].dtype),
            pltpu.SemaphoreType.DMA((slots,)),
            *extra,
        ],
    )(*(in_hbm(a) for a in parts), *args)


def cross_product(values):
    return lax.dot_general(
        values, values, (((0,), (0,)), ((), ())), preferred_element_type=jnp.float32
    )


def row_product(values):
    return lax.dot_general(
        values, values, (((1,), (1,)), ((), ())), preferred_element_type=jnp.float32
    )


def swap(values, axis, size, mask):
    return lax.ppermute(values, axis, [(i, i ^ mask) for i in range(size)])


def halve(values, axis, size, mask, dim=0):
    half = values.shape[dim] // 2
    bit = (lax.axis_index(axis) & mask) // mask
    kept = lax.dynamic_slice_in_dim(values, bit * half, half, dim)
    sent = lax.dynamic_slice_in_dim(values, (1 - bit) * half, half, dim)
    return kept + swap(sent, axis, size, mask)


def in_order(own, other, axis, mask):
    bit = (lax.axis_index(axis) & mask) // mask
    return jnp.where(
        bit == 0, jnp.concatenate([own, other], 0), jnp.concatenate([other, own], 0)
    )


def double(values, axis, size, mask):
    return in_order(values, swap(values, axis, size, mask), axis, mask)


def tree_sum(terms):
    while len(terms) > 1:
        terms = [terms[i] + terms[i + 1] for i in range(0, len(terms), 2)]
    return terms[0]


def masks_of(size):
    return [1 << b for b in range(size.bit_length() - 1)]


def spread(values, axis, size, step=1):
    return [values] + [swap(values, axis, size, d) for d in range(step, size, step)]


def all_sum(values, axis, size, step=1):
    return tree_sum(spread(values, axis, size, step))


def share_sum(values, axis, size):
    rows = values.shape[0] // size
    own = lax.axis_index(axis)

    def share(index):
        return lax.dynamic_slice_in_dim(values, index * rows, rows, 0)

    return tree_sum(
        [share(own)] + [swap(share(own ^ d), axis, size, d) for d in range(1, size)]
    )


def collect(values, axis, size):
    pieces = spread(values, axis, size)
    for mask in masks_of(size):
        pieces = [
            in_order(pieces[i], pieces[i + 1], axis, mask) for i in range(0, len(pieces), 2)
        ]
    return pieces[0]


def full_dot(left, right, dims):
    return lax.dot_general(
        left, right, (dims, ((), ())), precision=lax.Precision.HIGHEST,
        preferred_element_type=jnp.float32,
    )


def on_device(
    size_i, size_j, size_k, tensor, matrix, first_factor, second_factor, time_factor, column_factor
):
    f32 = jnp.float32
    tile_i, tile_j, tile_k = tensor.shape
    rank = first_factor.shape[1]
    half_rank = rank // 2
    share = half_rank // size_k
    core = lax.axis_index("ja") % 2
    along = lax.axis_index("ka") * share
    part = core * half_rank + along

    grams, gram_time, coupled, second_near, time_near = local_products(
        column_factor, second_factor, time_factor, matrix
    )
    grams = halve(grams, "ja", size_j, 1)
    gram_second = lax.dynamic_slice_in_dim(grams[:, rank:], along, share, 0)
    time_rows = lax.dynamic_slice_in_dim(gram_time, core * half_rank, half_rank, 0)
    grams = share_sum(jnp.concatenate([grams[:, :rank], time_rows], 1), "ka", size_k)
    time_rows = grams[:, rank:]
    grams = all_sum(jnp.concatenate([grams[:, :rank], gram_second], 1), "ja", size_j, 2)
    gram_column, gram_second = grams[:, :rank], grams[:, rank:]
    gram_column = all_sum(gram_column, "ia", size_i)
    gram_total = gram_second * time_rows + gram_column
    first_wide = first_factor.astype(f32)
    denominator = full_dot(gram_total, first_wide, ((1,), (1,)))

    for mask in reversed(masks_of(size_i)):
        coupled = halve(coupled, "ia", size_i, mask, 1)
    half = tile_j // 2
    slab, low = slab_and_turn(tensor, second_near, time_near, 0, half)
    slab, high = slab_and_turn(tensor, second_near, time_near, half, half, (slab,))
    turned = (low, high)
    numerator = slab + coupled
    numerator = halve(numerator, "ja", size_j, 1)
    numerator = share_sum(numerator, "ka", size_k)
    numerator = all_sum(numerator, "ja", size_j, 2)
    own = lax.dynamic_slice_in_dim(first_wide.T, part, share, 0)
    first_new = (own * numerator / denominator).astype(jnp.bfloat16)
    first_new = collect(first_new, "ka", size_k)
    first_new = double(first_new, "ja", size_j, 1)

    firsts = spread(first_new, "ia", size_i)
    gram_first = tree_sum([row_product(piece) for piece in firsts])
    times = time_factor
    for mask in masks_of(size_k):
        times = double(times, "ka", size_k, mask)
    gram_time = cross_product(times)
    plane_sum, first_out = weighted_call(
        plane_kernel,
        turned,
        (first_new, time_factor),
        (
            jax.ShapeDtypeStruct((tile_j, rank), f32),
            jax.ShapeDtypeStruct((tile_i, rank), jnp.bfloat16),
        ),
    )
    plane_sum = share_sum(plane_sum, "ka", size_k)
    plane_sum = all_sum(plane_sum, "ia", size_i)
    rows = tile_j // size_k
    own = lax.dynamic_slice_in_dim(second_factor, lax.axis_index("ka") * rows, rows, 0).astype(f32)
    denominator = full_dot(own, gram_first * gram_time, ((1,), (0,)))
    second_new = (own * plane_sum / denominator).astype(jnp.bfloat16)
    second_new = collect(second_new, "ka", size_k)

    seconds = second_new
    for mask in reversed(masks_of(size_j)):
        seconds = double(seconds, "ja", size_j, mask)
    gram_new = cross_product(seconds)
    (time_sum,) = weighted_call(
        time_kernel,
        turned,
        (first_new, second_new),
        (jax.ShapeDtypeStruct((tile_k, rank), f32),),
        (
            pltpu.VMEM((tile_j, rank), f32),
            pltpu.VMEM((tile_i, rank), jnp.bfloat16),
        ),
    )
    time_sum = halve(time_sum, "ja", size_j, 1)
    time_sum = all_sum(time_sum, ("ia", "ja"), size_i * size_j, 2)
    rows = tile_k // 2
    own = lax.dynamic_slice_in_dim(
        time_factor, (lax.axis_index("ja") % 2) * rows, rows, 0
    ).astype(f32)
    denominator = full_dot(own, gram_first * gram_new, ((1,), (0,)))
    time_new = (own * time_sum / denominator).astype(jnp.bfloat16)
    time_new = double(time_new, "ja", size_j, 1)
    return (first_out, second_new, time_new)


def in_layer(sizes, *args):
    return on_device(*sizes, *args)


def solution(mesh):
    sizes = (mesh.shape["ia"], mesh.shape["ja"], mesh.shape["ka"])
    return jax.shard_map(
        functools.partial(in_layer, sizes),
        mesh=mesh,
        in_specs=(
            P("ia", "ja", "ka"),
            P(None, ("ia", "ja", "ka")),
            P("ia", None),
            P("ja", None),
            P("ka", None),
            P(("ia", "ja", "ka"), None),
        ),
        out_specs=(P("ia", None), P("ja", None), P("ka", None)),
        check_vma=False,
    )
```

```python
import functools

import jax
import jax.numpy as jnp
from jax import lax
from jax.experimental import pallas as pl
from jax.experimental.pallas import tpu as pltpu
from jax.sharding import PartitionSpec as P


ANY = pl.BlockSpec(memory_space=pl.ANY)
VMEM = pl.BlockSpec(memory_space=pltpu.VMEM)
LIMIT = 32 << 20


def in_hbm(values):
    return pltpu.with_memory_space_constraint(values, pltpu.HBM)


def chunk_of(length, most):
    size = min(length, most)
    while length % size:
        size //= 2
    return size


def kernel_call(kernel, flops, nbytes, **kwargs):
    return pl.pallas_call(
        kernel,
        cost_estimate=pl.CostEstimate(flops=flops, bytes_accessed=nbytes, transcendentals=0),
        compiler_params=pltpu.CompilerParams(vmem_limit_bytes=LIMIT),
        **kwargs,
    )


def bring(sources, targets, sem):
    def copy(index):
        return pltpu.make_async_copy(sources[index], targets[index], sem.at[index])

    for index in range(len(sources)):
        copy(index).start()
    return lambda index: copy(index).wait()


def local_kernel(
    column, second, time, matrix, grams, gram_time, coupled, second_out, time_out, *scratch
):
    f32 = jnp.float32
    held, held_matrix, turned, sem = scratch
    targets = (held, second_out, time_out, held_matrix)
    wait = bring((column, second, time, matrix), targets, sem)
    rank = column.shape[1]
    wait(0)
    turned[...] = held[...].T
    grams[:, :rank] = jnp.dot(turned[...], held[...], preferred_element_type=f32)
    wait(1)
    grams[:, rank:] = jnp.dot(second_out[...].T, second_out[...], preferred_element_type=f32)
    wait(2)
    gram_time[...] = jnp.dot(time_out[...].T, time_out[...], preferred_element_type=f32)
    wait(3)
    coupled[...] = lax.dot_general(
        turned[...], held_matrix[...], (((1,), (1,)), ((), ())), preferred_element_type=f32
    )


def local_products(column, second, time, matrix):
    width, rank = column.shape
    rows = matrix.shape[0]
    f32 = jnp.float32
    return kernel_call(
        local_kernel,
        2 * width * rank * (rank + rows),
        2 * width * (rank + rows),
        out_shape=(
            jax.ShapeDtypeStruct((rank, 2 * rank), f32),
            jax.ShapeDtypeStruct((rank, rank), f32),
            jax.ShapeDtypeStruct((rank, rows), f32),
            jax.ShapeDtypeStruct(second.shape, second.dtype),
            jax.ShapeDtypeStruct(time.shape, time.dtype),
        ),
        in_specs=[ANY] * 4,
        out_specs=(VMEM,) * 5,
        scratch_shapes=[
            pltpu.VMEM(column.shape, column.dtype),
            pltpu.VMEM(matrix.shape, matrix.dtype),
            pltpu.VMEM((rank, width), column.dtype),
            pltpu.SemaphoreType.DMA((4,)),
        ],
    )(*(in_hbm(a) for a in (column, second, time, matrix)))


def slab_kernel(first, chunk, steps, tensor, second, time, *refs):
    *start, total, turned, read, read_sem, ready, ready_sem, added = refs
    ahead = min(3, steps)

    def fetch(step):
        source = tensor.at[:, pl.ds(first + step * chunk, chunk)]
        return pltpu.make_async_copy(source, read.at[step], read_sem.at[step])

    def put(step):
        target = turned.at[pl.ds(step * chunk, chunk)]
        return pltpu.make_async_copy(ready.at[step], target, ready_sem.at[step])

    for step in range(ahead):
        fetch(step).start()
    time_wide = time[...].astype(jnp.float32)
    added[...] = start[0][...] if start else jnp.zeros_like(added)

    def body(step, carry):
        fetch(step).wait()

        @pl.when(step + ahead < steps)
        def _():
            fetch(step + ahead).start()

        block = jnp.swapaxes(read[step], 0, 1)
        for j in range(chunk):
            ready[step, j] = block[j].T
        put(step).start()
        row = pl.multiple_of(first + step * chunk, chunk)
        weights = second[pl.ds(row, chunk), :].astype(jnp.float32)
        khatri = jnp.concatenate(
            [(weights[j : j + 1, :] * time_wide).astype(jnp.bfloat16) for j in range(chunk)], 0
        )
        tiles = jnp.concatenate([block[j] for j in range(chunk)], 1)
        added[...] += jnp.dot(tiles, khatri, preferred_element_type=jnp.float32)
        return carry

    lax.fori_loop(0, steps, body, 0)
    total[...] = added[...].T if start else added[...]

    def finish(step, carry):
        put(step).wait()
        return carry

    lax.fori_loop(0, steps, finish, 0)


def slab_and_turn(tensor, second, time, first, count, start=()):
    tile_i, _, tile_k = tensor.shape
    rank = time.shape[1]
    chunk = chunk_of(count, 8)
    steps = count // chunk
    return kernel_call(
        functools.partial(slab_kernel, first, chunk, steps),
        2 * tile_i * count * tile_k * rank,
        4 * tile_i * count * tile_k,
        out_shape=(
            jax.ShapeDtypeStruct((rank, tile_i) if start else (tile_i, rank), jnp.float32),
            pltpu.HBM((count, tile_k, tile_i), tensor.dtype),
        ),
        in_specs=[ANY] + [VMEM] * (2 + len(start)),
        out_specs=(VMEM, ANY),
        scratch_shapes=[
            pltpu.VMEM((steps, tile_i, chunk, tile_k), tensor.dtype),
            pltpu.SemaphoreType.DMA((steps,)),
            pltpu.VMEM((steps, chunk, tile_k, tile_i), tensor.dtype),
            pltpu.SemaphoreType.DMA((steps,)),
            pltpu.VMEM((tile_i, rank), jnp.float32),
        ],
    )(in_hbm(tensor), second, time, *start)


def fetcher(parts, read, read_sem, chunk):
    steps = parts[0].shape[0] // chunk

    def fetch(part, step):
        source = parts[part].at[pl.ds(step * chunk, chunk)]
        slot = part * steps + step
        return pltpu.make_async_copy(source, read.at[slot], read_sem.at[slot])

    for part in range(len(parts)):
        for step in range(steps):
            fetch(part, step).start()
    return fetch, steps


def plane_kernel(chunk, parts, which, first_turned, time, total, *refs):
    *first_out, first, read, read_sem = refs
    steps = parts[0].shape[0] // chunk

    def fetch(part, step):
        source = parts[part].at[pl.ds(step * chunk, chunk)]
        return pltpu.make_async_copy(source, read.at[step], read_sem.at[step])

    for part in range(len(parts)):

        @pl.when(which[0] == part)
        def _():
            for step in range(steps):
                fetch(part, step).start()

    first[...] = first_turned[...].T
    shared = first[...]

    def body(step, carry):
        fetch(0, step).wait()
        sums = []
        for j in range(chunk):
            weighted = jnp.dot(read[step, j], shared, preferred_element_type=jnp.float32)
            scaled = weighted * time[...].astype(jnp.float32)
            sums.append(jnp.sum(scaled, axis=0, keepdims=True))
        row = pl.multiple_of(step * chunk, chunk)
        total[pl.ds(row, chunk), :] = jnp.concatenate(sums, 0)
        return carry

    lax.fori_loop(0, steps, body, 0)
    if first_out:
        first_out[0][...] = first[...]


def plane_sums(parts, which, first_turned, time, with_first):
    count, tile_k, tile_i = parts[0].shape
    rank = first_turned.shape[0]
    chunk = chunk_of(count, 16)
    steps = count // chunk

    def on_parts(*refs):
        plane_kernel(chunk, refs[: len(parts)], *refs[len(parts) :])

    outs = (jax.ShapeDtypeStruct((count, rank), jnp.float32),)
    if with_first:
        outs += (jax.ShapeDtypeStruct((tile_i, rank), first_turned.dtype),)
    return kernel_call(
        on_parts,
        2 * tile_i * count * tile_k * rank,
        2 * tile_i * count * tile_k,
        out_shape=outs,
        in_specs=[ANY] * len(parts) + [pl.BlockSpec(memory_space=pltpu.SMEM), VMEM, VMEM],
        out_specs=(VMEM,) * len(outs),
        scratch_shapes=[
            pltpu.VMEM((tile_i, rank), first_turned.dtype),
            pltpu.VMEM((steps, chunk, tile_k, tile_i), parts[0].dtype),
            pltpu.SemaphoreType.DMA((steps,)),
        ],
    )(*(in_hbm(a) for a in parts), which.reshape(1).astype(jnp.int32), first_turned, time)


def time_kernel(chunk, parts, first_turned, second, total, read, read_sem, wide, first):
    fetch, steps = fetcher(parts, read, read_sem, chunk)
    wide[...] = second[...].astype(jnp.float32)
    first[...] = first_turned[...].T
    total[...] = jnp.zeros_like(total)
    shared = first[...]
    for part in range(len(parts)):

        def body(step, carry):
            fetch(part, step).wait()
            slot = part * steps + step
            sums = total[...]
            for j in range(chunk):
                weighted = jnp.dot(read[slot, j], shared, preferred_element_type=jnp.float32)
                sums = sums + weighted * wide[pl.ds(slot * chunk + j, 1), :]
            total[...] = sums
            return carry

        lax.fori_loop(0, steps, body, 0)


def weighted_call(kernel, parts, args, outs, extra=()):
    count, tile_k, tile_i = parts[0].shape
    chunk = chunk_of(count, 16)
    slots = len(parts) * count // chunk
    rank = args[0].shape[0]

    def on_parts(*refs):
        kernel(chunk, refs[: len(parts)], *refs[len(parts) :])

    return kernel_call(
        on_parts,
        2 * tile_i * len(parts) * count * tile_k * rank,
        2 * tile_i * len(parts) * count * tile_k,
        out_shape=outs,
        in_specs=[ANY] * len(parts) + [VMEM] * len(args),
        out_specs=(VMEM,) * len(outs),
        scratch_shapes=[
            pltpu.VMEM((slots, chunk, tile_k, tile_i), parts[0].dtype),
            pltpu.SemaphoreType.DMA((slots,)),
            *extra,
        ],
    )(*(in_hbm(a) for a in parts), *args)


def cross_product(values):
    return lax.dot_general(
        values, values, (((0,), (0,)), ((), ())), preferred_element_type=jnp.float32
    )


def row_product(values):
    return lax.dot_general(
        values, values, (((1,), (1,)), ((), ())), preferred_element_type=jnp.float32
    )


def swap(values, axis, size, mask):
    return lax.ppermute(values, axis, [(i, i ^ mask) for i in range(size)])


def halve(values, axis, size, mask, dim=0):
    half = values.shape[dim] // 2
    bit = (lax.axis_index(axis) & mask) // mask
    kept = lax.dynamic_slice_in_dim(values, bit * half, half, dim)
    sent = lax.dynamic_slice_in_dim(values, (1 - bit) * half, half, dim)
    return kept + swap(sent, axis, size, mask)


def in_order(own, other, axis, mask):
    bit = (lax.axis_index(axis) & mask) // mask
    return jnp.where(
        bit == 0, jnp.concatenate([own, other], 0), jnp.concatenate([other, own], 0)
    )


def double(values, axis, size, mask):
    return in_order(values, swap(values, axis, size, mask), axis, mask)


def tree_sum(terms):
    while len(terms) > 1:
        terms = [terms[i] + terms[i + 1] for i in range(0, len(terms), 2)]
    return terms[0]


def masks_of(size):
    return [1 << b for b in range(size.bit_length() - 1)]


def spread(values, axis, size, step=1):
    return [values] + [swap(values, axis, size, d) for d in range(step, size, step)]


def all_sum(values, axis, size, step=1):
    return tree_sum(spread(values, axis, size, step))


def full_dot(left, right, dims):
    return lax.dot_general(
        left, right, (dims, ((), ())), precision=lax.Precision.HIGHEST,
        preferred_element_type=jnp.float32,
    )


def on_device(
    size_i, size_j, size_k, tensor, matrix, first_factor, second_factor, time_factor, column_factor
):
    f32 = jnp.float32
    tile_i, tile_j, tile_k = tensor.shape
    rank = first_factor.shape[1]
    share = rank // size_j
    part = 0
    for mask in masks_of(size_j):
        part = 2 * part + (lax.axis_index("ja") & mask) // mask

    grams, gram_time, coupled, second_near, time_near = local_products(
        column_factor, second_factor, time_factor, matrix
    )
    for mask in masks_of(size_j):
        grams = halve(grams, "ja", size_j, mask)
    gram_second = grams[:, rank:]
    time_rows = lax.dynamic_slice_in_dim(gram_time, part * share, share, 0)
    grams = jnp.concatenate([grams[:, :rank], time_rows], 1)
    grams = all_sum(grams, "ka", size_k)
    gram_column, time_rows = grams[:, :rank], grams[:, rank:]
    gram_column = all_sum(gram_column, "ia", size_i)
    gram_total = gram_second * time_rows + gram_column
    first_wide = first_factor.astype(f32)
    denominator = full_dot(gram_total, first_wide, ((1,), (1,)))

    for mask in reversed(masks_of(size_i)):
        coupled = halve(coupled, "ia", size_i, mask, 1)
    half = tile_j // 2
    slab, low = slab_and_turn(tensor, second_near, time_near, 0, half)
    slab, high = slab_and_turn(tensor, second_near, time_near, half, half, (slab,))
    turned = (low, high)
    numerator = slab + coupled
    for mask in masks_of(size_j):
        numerator = halve(numerator, "ja", size_j, mask)
    numerator = all_sum(numerator, "ka", size_k)
    own = lax.dynamic_slice_in_dim(first_wide.T, part * share, share, 0)
    first_new = (own * numerator / denominator).astype(jnp.bfloat16)
    pieces = spread(first_new, "ja", size_j)
    for mask in reversed(masks_of(size_j)):
        pieces = [in_order(pieces[d], pieces[d + mask], "ja", mask) for d in range(mask)]
    first_new = pieces[0]

    firsts = spread(first_new, "ia", size_i)
    gram_first = tree_sum([row_product(piece) for piece in firsts])
    times = time_factor
    for mask in masks_of(size_k):
        times = double(times, "ka", size_k, mask)
    gram_time = cross_product(times)
    upper, *lower = reversed(masks_of(size_i))
    bit = (lax.axis_index("ia") & upper) // upper
    (sent,) = plane_sums(turned, 1 - bit, first_new, time_factor, False)
    came = swap(sent, "ia", size_i, upper)
    kept, first_out = plane_sums(turned, bit, first_new, time_factor, True)
    plane_sum = kept + came
    for mask in lower:
        plane_sum = halve(plane_sum, "ia", size_i, mask)
    plane_sum = all_sum(plane_sum, "ka", size_k)
    rows = tile_j // size_i
    own = lax.dynamic_slice_in_dim(second_factor, lax.axis_index("ia") * rows, rows, 0).astype(f32)
    denominator = full_dot(own, gram_first * gram_time, ((1,), (0,)))
    second_new = (own * plane_sum / denominator).astype(jnp.bfloat16)
    for mask in masks_of(size_i):
        second_new = double(second_new, "ia", size_i, mask)

    seconds = second_new
    for mask in reversed(masks_of(size_j)):
        seconds = double(seconds, "ja", size_j, mask)
    gram_new = cross_product(seconds)
    (time_sum,) = weighted_call(
        time_kernel,
        turned,
        (first_new, second_new),
        (jax.ShapeDtypeStruct((tile_k, rank), f32),),
        (
            pltpu.VMEM((tile_j, rank), f32),
            pltpu.VMEM((tile_i, rank), jnp.bfloat16),
        ),
    )
    time_sum = halve(time_sum, "ja", size_j, 1)
    time_sum = all_sum(time_sum, ("ia", "ja"), size_i * size_j, 2)
    rows = tile_k // 2
    own = lax.dynamic_slice_in_dim(
        time_factor, (lax.axis_index("ja") % 2) * rows, rows, 0
    ).astype(f32)
    denominator = full_dot(own, gram_first * gram_new, ((1,), (0,)))
    time_new = (own * time_sum / denominator).astype(jnp.bfloat16)
    time_new = double(time_new, "ja", size_j, 1)
    return (first_out, second_new, time_new)


def in_layer(sizes, *args):
    return on_device(*sizes, *args)


def solution(mesh):
    sizes = (mesh.shape["ia"], mesh.shape["ja"], mesh.shape["ka"])
    return jax.shard_map(
        functools.partial(in_layer, sizes),
        mesh=mesh,
        in_specs=(
            P("ia", "ja", "ka"),
            P(None, ("ia", "ja", "ka")),
            P("ia", None),
            P("ja", None),
            P("ka", None),
            P(("ia", "ja", "ka"), None),
        ),
        out_specs=(P("ia", None), P("ja", None), P("ka", None)),
        check_vma=False,
    )
```

```python
import functools

import jax
import jax.numpy as jnp
from jax import lax
from jax.experimental import pallas as pl
from jax.experimental.pallas import tpu as pltpu
from jax.sharding import PartitionSpec as P


ANY = pl.BlockSpec(memory_space=pl.ANY)
VMEM = pl.BlockSpec(memory_space=pltpu.VMEM)
LIMIT = 32 << 20


def in_hbm(values):
    return pltpu.with_memory_space_constraint(values, pltpu.HBM)


def chunk_of(length, most):
    size = min(length, most)
    while length % size:
        size //= 2
    return size


def kernel_call(kernel, flops, nbytes, **kwargs):
    return pl.pallas_call(
        kernel,
        cost_estimate=pl.CostEstimate(flops=flops, bytes_accessed=nbytes, transcendentals=0),
        compiler_params=pltpu.CompilerParams(vmem_limit_bytes=LIMIT),
        **kwargs,
    )


def bring(sources, targets, sem):
    def copy(index):
        return pltpu.make_async_copy(sources[index], targets[index], sem.at[index])

    for index in range(len(sources)):
        copy(index).start()
    return lambda index: copy(index).wait()


def local_kernel(
    column, second, time, matrix, grams, gram_time, coupled, second_out, time_out, *scratch
):
    f32 = jnp.float32
    held, held_matrix, turned, sem = scratch
    targets = (held, second_out, time_out, held_matrix)
    wait = bring((column, second, time, matrix), targets, sem)
    rank = column.shape[1]
    wait(0)
    turned[...] = held[...].T
    grams[:, :rank] = jnp.dot(turned[...], held[...], preferred_element_type=f32)
    wait(1)
    grams[:, rank:] = jnp.dot(second_out[...].T, second_out[...], preferred_element_type=f32)
    wait(2)
    gram_time[...] = jnp.dot(time_out[...].T, time_out[...], preferred_element_type=f32)
    wait(3)
    coupled[...] = lax.dot_general(
        turned[...], held_matrix[...], (((1,), (1,)), ((), ())), preferred_element_type=f32
    )


def local_products(column, second, time, matrix):
    width, rank = column.shape
    rows = matrix.shape[0]
    f32 = jnp.float32
    return kernel_call(
        local_kernel,
        2 * width * rank * (rank + rows),
        2 * width * (rank + rows),
        out_shape=(
            jax.ShapeDtypeStruct((rank, 2 * rank), f32),
            jax.ShapeDtypeStruct((rank, rank), f32),
            jax.ShapeDtypeStruct((rank, rows), f32),
            jax.ShapeDtypeStruct(second.shape, second.dtype),
            jax.ShapeDtypeStruct(time.shape, time.dtype),
        ),
        in_specs=[ANY] * 4,
        out_specs=(VMEM,) * 5,
        scratch_shapes=[
            pltpu.VMEM(column.shape, column.dtype),
            pltpu.VMEM(matrix.shape, matrix.dtype),
            pltpu.VMEM((rank, width), column.dtype),
            pltpu.SemaphoreType.DMA((4,)),
        ],
    )(*(in_hbm(a) for a in (column, second, time, matrix)))


def slab_kernel(first, chunk, steps, tensor, second, time, *refs):
    *start, total, turned, read, read_sem, ready, ready_sem, added = refs
    ahead = min(4, steps)

    def fetch(step):
        source = tensor.at[:, pl.ds(first + step * chunk, chunk)]
        return pltpu.make_async_copy(source, read.at[step], read_sem.at[step])

    def put(step):
        target = turned.at[pl.ds(step * chunk, chunk)]
        return pltpu.make_async_copy(ready.at[step], target, ready_sem.at[step])

    for step in range(ahead):
        fetch(step).start()
    time_wide = time[...].astype(jnp.float32)
    added[...] = start[0][...] if start else jnp.zeros_like(added)

    def body(step, carry):
        fetch(step).wait()

        @pl.when(step + ahead < steps)
        def _():
            fetch(step + ahead).start()

        block = jnp.swapaxes(read[step], 0, 1)
        for j in range(chunk):
            ready[step, j] = block[j].T
        put(step).start()
        row = pl.multiple_of(first + step * chunk, chunk)
        weights = second[pl.ds(row, chunk), :].astype(jnp.float32)
        khatri = jnp.concatenate(
            [(weights[j : j + 1, :] * time_wide).astype(jnp.bfloat16) for j in range(chunk)], 0
        )
        tiles = jnp.concatenate([block[j] for j in range(chunk)], 1)
        added[...] += jnp.dot(tiles, khatri, preferred_element_type=jnp.float32)
        return carry

    lax.fori_loop(0, steps, body, 0)
    total[...] = added[...].T if start else added[...]

    def finish(step, carry):
        put(step).wait()
        return carry

    lax.fori_loop(0, steps, finish, 0)


def slab_and_turn(tensor, second, time, first, count, start=()):
    tile_i, _, tile_k = tensor.shape
    rank = time.shape[1]
    chunk = chunk_of(count, 8)
    steps = count // chunk
    return kernel_call(
        functools.partial(slab_kernel, first, chunk, steps),
        2 * tile_i * count * tile_k * rank,
        4 * tile_i * count * tile_k,
        out_shape=(
            jax.ShapeDtypeStruct((rank, tile_i) if start else (tile_i, rank), jnp.float32),
            pltpu.HBM((count, tile_k, tile_i), tensor.dtype),
        ),
        in_specs=[ANY] + [VMEM] * (2 + len(start)),
        out_specs=(VMEM, ANY),
        scratch_shapes=[
            pltpu.VMEM((steps, tile_i, chunk, tile_k), tensor.dtype),
            pltpu.SemaphoreType.DMA((steps,)),
            pltpu.VMEM((steps, chunk, tile_k, tile_i), tensor.dtype),
            pltpu.SemaphoreType.DMA((steps,)),
            pltpu.VMEM((tile_i, rank), jnp.float32),
        ],
    )(in_hbm(tensor), second, time, *start)


def fetch_part(parts, which, read, read_sem, chunk):
    steps = read.shape[0]

    def copy(part, step):
        source = parts[part].at[pl.ds(step * chunk, chunk)]
        return pltpu.make_async_copy(source, read.at[step], read_sem.at[step])

    for part in range(len(parts)):

        @pl.when(which[0] == part)
        def _():
            for step in range(steps):
                copy(part, step).start()

    return lambda step: copy(0, step).wait()


def plane_kernel(chunk, parts, which, first_turned, time, total, first, read, read_sem):
    wait = fetch_part(parts, which, read, read_sem, chunk)
    first[...] = first_turned[...].T
    shared = first[...]

    def body(step, carry):
        wait(step)
        sums = []
        for j in range(chunk):
            weighted = jnp.dot(read[step, j], shared, preferred_element_type=jnp.float32)
            scaled = weighted * time[...].astype(jnp.float32)
            sums.append(jnp.sum(scaled, axis=0, keepdims=True))
        row = pl.multiple_of(step * chunk, chunk)
        total[pl.ds(row, chunk), :] = jnp.concatenate(sums, 0)
        return carry

    lax.fori_loop(0, read.shape[0], body, 0)


def time_kernel(chunk, parts, which, first_turned, second, *refs):
    *start, total, first, read, read_sem, wide = refs
    wait = fetch_part(parts, which, read, read_sem, chunk)
    wide[...] = second[...].astype(jnp.float32)
    first[...] = first_turned[...].T
    total[...] = start[0][...] if start else jnp.zeros_like(total)
    shared = first[...]

    def body(step, carry):
        wait(step)
        sums = total[...]
        for j in range(chunk):
            weighted = jnp.dot(read[step, j], shared, preferred_element_type=jnp.float32)
            sums = sums + weighted * wide[pl.ds(step * chunk + j, 1), :]
        total[...] = sums
        return carry

    lax.fori_loop(0, read.shape[0], body, 0)


def weighted_call(kernel, parts, which, args, out_rows, extra=()):
    count, tile_k, tile_i = parts[0].shape
    rank = args[0].shape[0]
    chunk = chunk_of(count, 16)
    steps = count // chunk

    def on_parts(*refs):
        kernel(chunk, refs[: len(parts)], *refs[len(parts) :])

    return kernel_call(
        on_parts,
        2 * tile_i * count * tile_k * rank,
        2 * tile_i * count * tile_k,
        out_shape=jax.ShapeDtypeStruct((out_rows, rank), jnp.float32),
        in_specs=[ANY] * len(parts)
        + [pl.BlockSpec(memory_space=pltpu.SMEM)]
        + [VMEM] * len(args),
        out_specs=VMEM,
        scratch_shapes=[
            pltpu.VMEM((tile_i, rank), args[0].dtype),
            pltpu.VMEM((steps, chunk, tile_k, tile_i), parts[0].dtype),
            pltpu.SemaphoreType.DMA((steps,)),
            *extra,
        ],
    )(*(in_hbm(a) for a in parts), which.reshape(1).astype(jnp.int32), *args)


def cross_product(values):
    return lax.dot_general(
        values, values, (((0,), (0,)), ((), ())), preferred_element_type=jnp.float32
    )


def row_product(values):
    return lax.dot_general(
        values, values, (((1,), (1,)), ((), ())), preferred_element_type=jnp.float32
    )


def swap(values, axis, size, mask):
    return lax.ppermute(values, axis, [(i, i ^ mask) for i in range(size)])


def halve(values, axis, size, mask, dim=0):
    half = values.shape[dim] // 2
    bit = (lax.axis_index(axis) & mask) // mask
    kept = lax.dynamic_slice_in_dim(values, bit * half, half, dim)
    sent = lax.dynamic_slice_in_dim(values, (1 - bit) * half, half, dim)
    return kept + swap(sent, axis, size, mask)


def in_order(own, other, axis, mask):
    bit = (lax.axis_index(axis) & mask) // mask
    return jnp.where(
        bit == 0, jnp.concatenate([own, other], 0), jnp.concatenate([other, own], 0)
    )


def double(values, axis, size, mask):
    return in_order(values, swap(values, axis, size, mask), axis, mask)


def tree_sum(terms):
    while len(terms) > 1:
        terms = [terms[i] + terms[i + 1] for i in range(0, len(terms), 2)]
    return terms[0]


def masks_of(size):
    return [1 << b for b in range(size.bit_length() - 1)]


def spread(values, axis, size, step=1):
    return [values] + [swap(values, axis, size, d) for d in range(step, size, step)]


def all_sum(values, axis, size, step=1):
    return tree_sum(spread(values, axis, size, step))


def full_dot(left, right, dims):
    return lax.dot_general(
        left, right, (dims, ((), ())), precision=lax.Precision.HIGHEST,
        preferred_element_type=jnp.float32,
    )


def on_device(
    size_i, size_j, size_k, tensor, matrix, first_factor, second_factor, time_factor, column_factor
):
    f32 = jnp.float32
    _, tile_j, tile_k = tensor.shape
    rank = first_factor.shape[1]
    share = rank // size_j

    def part_of(place):
        part = 0
        for mask in masks_of(size_j):
            part = 2 * part + (place & mask) // mask
        return part

    part = part_of(lax.axis_index("ja"))

    grams, gram_time, coupled, second_near, time_near = local_products(
        column_factor, second_factor, time_factor, matrix
    )
    for mask in masks_of(size_j):
        grams = halve(grams, "ja", size_j, mask)
    gram_second = grams[:, rank:]
    time_rows = lax.dynamic_slice_in_dim(gram_time, part * share, share, 0)
    grams = jnp.concatenate([grams[:, :rank], time_rows], 1)
    grams = all_sum(grams, "ka", size_k)
    gram_column, time_rows = grams[:, :rank], grams[:, rank:]
    gram_column = all_sum(gram_column, "ia", size_i)
    gram_total = gram_second * time_rows + gram_column
    first_wide = first_factor.astype(f32)
    denominator = full_dot(gram_total, first_wide, ((1,), (1,)))

    for mask in reversed(masks_of(size_i)):
        coupled = halve(coupled, "ia", size_i, mask, 1)
    half = tile_j // 2
    slab, low = slab_and_turn(tensor, second_near, time_near, 0, half)
    slab, high = slab_and_turn(tensor, second_near, time_near, half, half, (slab,))
    turned = (low, high)
    numerator = slab + coupled
    place = lax.axis_index("ja")
    pieces = [lax.dynamic_slice_in_dim(numerator, part * share, share, 0)]
    for d in range(1, size_j):
        sent = lax.dynamic_slice_in_dim(numerator, part_of(place ^ d) * share, share, 0)
        pieces.append(swap(sent, "ja", size_j, d))
    numerator = tree_sum(pieces)
    numerator = all_sum(numerator, "ka", size_k)
    own = lax.dynamic_slice_in_dim(first_wide.T, part * share, share, 0)
    first_new = (own * numerator / denominator).astype(jnp.bfloat16)
    pieces = spread(first_new, "ja", size_j)
    for mask in reversed(masks_of(size_j)):
        pieces = [in_order(pieces[d], pieces[d + mask], "ja", mask) for d in range(mask)]
    first_new = pieces[0]

    firsts = spread(first_new, "ia", size_i)
    gram_first = tree_sum([row_product(piece) for piece in firsts])
    times = time_factor
    for mask in masks_of(size_k):
        times = double(times, "ka", size_k, mask)
    gram_time = cross_product(times)
    upper, *lower = reversed(masks_of(size_i))
    bit = (lax.axis_index("ia") & upper) // upper
    plane_args = ((first_new, time_factor), half)
    sent = weighted_call(plane_kernel, turned, 1 - bit, *plane_args)
    came = swap(sent, "ia", size_i, upper)
    kept = weighted_call(plane_kernel, turned, bit, *plane_args)
    plane_sum = kept + came
    for mask in lower:
        plane_sum = halve(plane_sum, "ia", size_i, mask)
    plane_sum = all_sum(plane_sum, "ka", size_k)
    rows = tile_j // size_i
    own = lax.dynamic_slice_in_dim(second_factor, lax.axis_index("ia") * rows, rows, 0).astype(f32)
    denominator = full_dot(own, gram_first * gram_time, ((1,), (0,)))
    second_new = (own * plane_sum / denominator).astype(jnp.bfloat16)
    for mask in reversed(lower):
        second_new = double(second_new, "ia", size_i, mask)
    other = swap(second_new, "ia", size_i, upper)
    wide = (pltpu.VMEM((half, rank), f32),)
    time_sum = weighted_call(time_kernel, turned, bit, (first_new, second_new), tile_k, wide)
    time_sum = weighted_call(
        time_kernel, turned, 1 - bit, (first_new, other, time_sum), tile_k, wide
    )
    second_new = in_order(second_new, other, "ia", upper)

    seconds = second_new
    for mask in reversed(masks_of(size_j)):
        seconds = double(seconds, "ja", size_j, mask)
    gram_new = cross_product(seconds)
    time_sum = halve(time_sum, "ja", size_j, 1)
    time_sum = all_sum(time_sum, ("ia", "ja"), size_i * size_j, 2)
    rows = tile_k // 2
    own = lax.dynamic_slice_in_dim(
        time_factor, (lax.axis_index("ja") % 2) * rows, rows, 0
    ).astype(f32)
    denominator = full_dot(own, gram_first * gram_new, ((1,), (0,)))
    time_new = (own * time_sum / denominator).astype(jnp.bfloat16)
    time_new = double(time_new, "ja", size_j, 1)
    first_out = first_new.T
    return (first_out, second_new, time_new)


def in_layer(sizes, *args):
    return on_device(*sizes, *args)


def solution(mesh):
    sizes = (mesh.shape["ia"], mesh.shape["ja"], mesh.shape["ka"])
    return jax.shard_map(
        functools.partial(in_layer, sizes),
        mesh=mesh,
        in_specs=(
            P("ia", "ja", "ka"),
            P(None, ("ia", "ja", "ka")),
            P("ia", None),
            P("ja", None),
            P("ka", None),
            P(("ia", "ja", "ka"), None),
        ),
        out_specs=(P("ia", None), P("ja", None), P("ka", None)),
        check_vma=False,
    )
```

```python
import functools

import jax
import jax.numpy as jnp
from jax import lax
from jax.experimental import pallas as pl
from jax.experimental.pallas import tpu as pltpu
from jax.sharding import PartitionSpec as P


ANY = pl.BlockSpec(memory_space=pl.ANY)
VMEM = pl.BlockSpec(memory_space=pltpu.VMEM)
LIMIT = 32 << 20


def in_hbm(values):
    return pltpu.with_memory_space_constraint(values, pltpu.HBM)


def chunk_of(length, most):
    size = min(length, most)
    while length % size:
        size //= 2
    return size


def kernel_call(kernel, flops, nbytes, **kwargs):
    return pl.pallas_call(
        kernel,
        cost_estimate=pl.CostEstimate(flops=flops, bytes_accessed=nbytes, transcendentals=0),
        compiler_params=pltpu.CompilerParams(vmem_limit_bytes=LIMIT),
        **kwargs,
    )


def bring(sources, targets, sem):
    def copy(index):
        return pltpu.make_async_copy(sources[index], targets[index], sem.at[index])

    for index in range(len(sources)):
        copy(index).start()
    return lambda index: copy(index).wait()


def local_kernel(
    column, second, time, matrix, grams, gram_time, coupled, second_out, time_out, *scratch
):
    f32 = jnp.float32
    held, held_matrix, turned, sem = scratch
    targets = (held, second_out, time_out, held_matrix)
    wait = bring((column, second, time, matrix), targets, sem)
    rank = column.shape[1]
    wait(0)
    turned[...] = held[...].T
    grams[:, :rank] = jnp.dot(turned[...], held[...], preferred_element_type=f32)
    wait(1)
    grams[:, rank:] = jnp.dot(second_out[...].T, second_out[...], preferred_element_type=f32)
    wait(2)
    gram_time[...] = jnp.dot(time_out[...].T, time_out[...], preferred_element_type=f32)
    wait(3)
    coupled[...] = lax.dot_general(
        turned[...], held_matrix[...], (((1,), (1,)), ((), ())), preferred_element_type=f32
    )


def local_products(column, second, time, matrix):
    width, rank = column.shape
    rows = matrix.shape[0]
    f32 = jnp.float32
    return kernel_call(
        local_kernel,
        2 * width * rank * (rank + rows),
        2 * width * (rank + rows),
        out_shape=(
            jax.ShapeDtypeStruct((rank, 2 * rank), f32),
            jax.ShapeDtypeStruct((rank, rank), f32),
            jax.ShapeDtypeStruct((rank, rows), f32),
            jax.ShapeDtypeStruct(second.shape, second.dtype),
            jax.ShapeDtypeStruct(time.shape, time.dtype),
        ),
        in_specs=[ANY] * 4,
        out_specs=(VMEM,) * 5,
        scratch_shapes=[
            pltpu.VMEM(column.shape, column.dtype),
            pltpu.VMEM(matrix.shape, matrix.dtype),
            pltpu.VMEM((rank, width), column.dtype),
            pltpu.SemaphoreType.DMA((4,)),
        ],
    )(*(in_hbm(a) for a in (column, second, time, matrix)))


def slab_kernel(first, chunk, steps, tensor, second, time, *refs):
    *start, total, turned, read, read_sem, ready, ready_sem, added = refs
    ahead = min(4, steps)

    def fetch(step):
        source = tensor.at[:, pl.ds(first + step * chunk, chunk)]
        return pltpu.make_async_copy(source, read.at[step], read_sem.at[step])

    def put(step):
        target = turned.at[pl.ds(step * chunk, chunk)]
        return pltpu.make_async_copy(ready.at[step], target, ready_sem.at[step])

    for step in range(ahead):
        fetch(step).start()
    time_wide = time[...].astype(jnp.float32)
    added[...] = start[0][...] if start else jnp.zeros_like(added)

    def body(step, carry):
        fetch(step).wait()

        @pl.when(step + ahead < steps)
        def _():
            fetch(step + ahead).start()

        block = jnp.swapaxes(read[step], 0, 1)
        for j in range(chunk):
            ready[step, j] = block[j].T
        put(step).start()
        row = pl.multiple_of(first + step * chunk, chunk)
        weights = second[pl.ds(row, chunk), :].astype(jnp.float32)
        khatri = jnp.concatenate(
            [(weights[j : j + 1, :] * time_wide).astype(jnp.bfloat16) for j in range(chunk)], 0
        )
        tiles = jnp.concatenate([block[j] for j in range(chunk)], 1)
        added[...] += jnp.dot(tiles, khatri, preferred_element_type=jnp.float32)
        return carry

    lax.fori_loop(0, steps, body, 0)
    total[...] = added[...].T if start else added[...]

    def finish(step, carry):
        put(step).wait()
        return carry

    lax.fori_loop(0, steps, finish, 0)


def slab_and_turn(tensor, second, time, first, count, start=()):
    tile_i, _, tile_k = tensor.shape
    rank = time.shape[1]
    chunk = chunk_of(count, 8)
    steps = count // chunk
    return kernel_call(
        functools.partial(slab_kernel, first, chunk, steps),
        2 * tile_i * count * tile_k * rank,
        4 * tile_i * count * tile_k,
        out_shape=(
            jax.ShapeDtypeStruct((rank, tile_i) if start else (tile_i, rank), jnp.float32),
            pltpu.HBM((count, tile_k, tile_i), tensor.dtype),
        ),
        in_specs=[ANY] + [VMEM] * (2 + len(start)),
        out_specs=(VMEM, ANY),
        scratch_shapes=[
            pltpu.VMEM((steps, tile_i, chunk, tile_k), tensor.dtype),
            pltpu.SemaphoreType.DMA((steps,)),
            pltpu.VMEM((steps, chunk, tile_k, tile_i), tensor.dtype),
            pltpu.SemaphoreType.DMA((steps,)),
            pltpu.VMEM((tile_i, rank), jnp.float32),
        ],
    )(in_hbm(tensor), second, time, *start)


def fetch_part(parts, which, read, read_sem, chunk):
    steps = read.shape[0]

    def copy(part, step):
        source = parts[part].at[pl.ds(step * chunk, chunk)]
        return pltpu.make_async_copy(source, read.at[step], read_sem.at[step])

    for part in range(len(parts)):

        @pl.when(which[0] == part)
        def _():
            for step in range(steps):
                copy(part, step).start()

    return lambda step: copy(0, step).wait()


def plane_kernel(chunk, parts, which, first_turned, time, total, first, read, read_sem):
    wait = fetch_part(parts, which, read, read_sem, chunk)
    first[...] = first_turned[...].T
    shared = first[...]

    def body(step, carry):
        wait(step)
        sums = []
        for j in range(chunk):
            weighted = jnp.dot(read[step, j], shared, preferred_element_type=jnp.float32)
            scaled = weighted * time[...].astype(jnp.float32)
            sums.append(jnp.sum(scaled, axis=0, keepdims=True))
        row = pl.multiple_of(step * chunk, chunk)
        total[pl.ds(row, chunk), :] = jnp.concatenate(sums, 0)
        return carry

    lax.fori_loop(0, read.shape[0], body, 0)


def time_kernel(chunk, parts, which, first_turned, second, *refs):
    *start, total, first, read, read_sem, wide = refs
    wait = fetch_part(parts, which, read, read_sem, chunk)
    wide[...] = second[...].astype(jnp.float32)
    first[...] = first_turned[...].T
    total[...] = start[0][...] if start else jnp.zeros_like(total)
    shared = first[...]

    def body(step, carry):
        wait(step)
        sums = total[...]
        for j in range(chunk):
            weighted = jnp.dot(read[step, j], shared, preferred_element_type=jnp.float32)
            sums = sums + weighted * wide[pl.ds(step * chunk + j, 1), :]
        total[...] = sums
        return carry

    lax.fori_loop(0, read.shape[0], body, 0)


def weighted_call(kernel, parts, which, args, out_rows, extra=()):
    count, tile_k, tile_i = parts[0].shape
    rank = args[0].shape[0]
    chunk = chunk_of(count, 16)
    steps = count // chunk

    def on_parts(*refs):
        kernel(chunk, refs[: len(parts)], *refs[len(parts) :])

    return kernel_call(
        on_parts,
        2 * tile_i * count * tile_k * rank,
        2 * tile_i * count * tile_k,
        out_shape=jax.ShapeDtypeStruct((out_rows, rank), jnp.float32),
        in_specs=[ANY] * len(parts)
        + [pl.BlockSpec(memory_space=pltpu.SMEM)]
        + [VMEM] * len(args),
        out_specs=VMEM,
        scratch_shapes=[
            pltpu.VMEM((tile_i, rank), args[0].dtype),
            pltpu.VMEM((steps, chunk, tile_k, tile_i), parts[0].dtype),
            pltpu.SemaphoreType.DMA((steps,)),
            *extra,
        ],
    )(*(in_hbm(a) for a in parts), which.reshape(1).astype(jnp.int32), *args)


def cross_product(values):
    return lax.dot_general(
        values, values, (((0,), (0,)), ((), ())), preferred_element_type=jnp.float32
    )


def row_product(values):
    return lax.dot_general(
        values, values, (((1,), (1,)), ((), ())), preferred_element_type=jnp.float32
    )


def swap(values, axis, size, mask):
    return lax.ppermute(values, axis, [(i, i ^ mask) for i in range(size)])


def halve(values, axis, size, mask, dim=0):
    half = values.shape[dim] // 2
    bit = (lax.axis_index(axis) & mask) // mask
    kept = lax.dynamic_slice_in_dim(values, bit * half, half, dim)
    sent = lax.dynamic_slice_in_dim(values, (1 - bit) * half, half, dim)
    return kept + swap(sent, axis, size, mask)


def in_order(own, other, axis, mask):
    bit = (lax.axis_index(axis) & mask) // mask
    return jnp.where(
        bit == 0, jnp.concatenate([own, other], 0), jnp.concatenate([other, own], 0)
    )


def double(values, axis, size, mask):
    return in_order(values, swap(values, axis, size, mask), axis, mask)


def tree_sum(terms):
    while len(terms) > 1:
        terms = [terms[i] + terms[i + 1] for i in range(0, len(terms), 2)]
    return terms[0]


def masks_of(size):
    return [1 << b for b in range(size.bit_length() - 1)]


def spread(values, axis, size, step=1):
    return [values] + [swap(values, axis, size, d) for d in range(step, size, step)]


def all_sum(values, axis, size, step=1):
    return tree_sum(spread(values, axis, size, step))


def far_sum(values, axis, size):
    terms = [values]
    for d in range(1, size):
        terms.append(swap(values, axis, size, d))
    return tree_sum(terms)


def full_dot(left, right, dims):
    return lax.dot_general(
        left, right, (dims, ((), ())), precision=lax.Precision.HIGHEST,
        preferred_element_type=jnp.float32,
    )


def on_device(
    size_i, size_j, size_k, tensor, matrix, first_factor, second_factor, time_factor, column_factor
):
    f32 = jnp.float32
    _, tile_j, tile_k = tensor.shape
    rank = first_factor.shape[1]
    share = rank // size_j

    def part_of(place):
        part = 0
        for mask in masks_of(size_j):
            part = 2 * part + (place & mask) // mask
        return part

    part = part_of(lax.axis_index("ja"))

    grams, gram_time, coupled, second_near, time_near = local_products(
        column_factor, second_factor, time_factor, matrix
    )
    for mask in masks_of(size_j):
        grams = halve(grams, "ja", size_j, mask)
    gram_second = grams[:, rank:]
    time_rows = lax.dynamic_slice_in_dim(gram_time, part * share, share, 0)
    grams = jnp.concatenate([grams[:, :rank], time_rows], 1)
    grams = far_sum(grams, "ka", size_k)
    gram_column, time_rows = grams[:, :rank], grams[:, rank:]
    gram_column = all_sum(gram_column, "ia", size_i)
    gram_total = gram_second * time_rows + gram_column
    first_wide = first_factor.astype(f32)
    denominator = full_dot(gram_total, first_wide, ((1,), (1,)))

    for mask in reversed(masks_of(size_i)):
        coupled = halve(coupled, "ia", size_i, mask, 1)
    half = tile_j // 2
    slab, low = slab_and_turn(tensor, second_near, time_near, 0, half)
    slab, high = slab_and_turn(tensor, second_near, time_near, half, half, (slab,))
    turned = (low, high)
    numerator = slab + coupled
    place = lax.axis_index("ja")
    pieces = [lax.dynamic_slice_in_dim(numerator, part * share, share, 0)]
    for d in range(1, size_j):
        sent = lax.dynamic_slice_in_dim(numerator, part_of(place ^ d) * share, share, 0)
        pieces.append(swap(sent, "ja", size_j, d))
    numerator = tree_sum(pieces)
    numerator = far_sum(numerator, "ka", size_k)
    own = lax.dynamic_slice_in_dim(first_wide.T, part * share, share, 0)
    first_new = (own * numerator / denominator).astype(jnp.bfloat16)
    pieces = spread(first_new, "ja", size_j)
    for mask in reversed(masks_of(size_j)):
        pieces = [in_order(pieces[d], pieces[d + mask], "ja", mask) for d in range(mask)]
    first_new = pieces[0]

    firsts = spread(first_new, "ia", size_i)
    gram_first = tree_sum([row_product(piece) for piece in firsts])
    times = time_factor
    for mask in masks_of(size_k):
        times = double(times, "ka", size_k, mask)
    gram_time = cross_product(times)
    upper, *lower = reversed(masks_of(size_i))
    bit = (lax.axis_index("ia") & upper) // upper
    plane_args = ((first_new, time_factor), half)
    sent = weighted_call(plane_kernel, turned, 1 - bit, *plane_args)
    came = swap(sent, "ia", size_i, upper)
    kept = weighted_call(plane_kernel, turned, bit, *plane_args)
    plane_sum = kept + came
    for mask in lower:
        plane_sum = halve(plane_sum, "ia", size_i, mask)
    plane_sum = far_sum(plane_sum, "ka", size_k)
    rows = tile_j // size_i
    own = lax.dynamic_slice_in_dim(second_factor, lax.axis_index("ia") * rows, rows, 0).astype(f32)
    denominator = full_dot(own, gram_first * gram_time, ((1,), (0,)))
    second_new = (own * plane_sum / denominator).astype(jnp.bfloat16)
    for mask in reversed(lower):
        second_new = double(second_new, "ia", size_i, mask)
    other = swap(second_new, "ia", size_i, upper)
    wide = (pltpu.VMEM((half, rank), f32),)
    time_sum = weighted_call(time_kernel, turned, bit, (first_new, second_new), tile_k, wide)
    time_sum = weighted_call(
        time_kernel, turned, 1 - bit, (first_new, other, time_sum), tile_k, wide
    )
    second_new = in_order(second_new, other, "ia", upper)

    seconds = second_new
    for mask in reversed(masks_of(size_j)):
        seconds = double(seconds, "ja", size_j, mask)
    gram_new = cross_product(seconds)
    time_sum = halve(time_sum, "ja", size_j, 1)
    time_sum = all_sum(time_sum, ("ia", "ja"), size_i * size_j, 2)
    rows = tile_k // 2
    own = lax.dynamic_slice_in_dim(
        time_factor, (lax.axis_index("ja") % 2) * rows, rows, 0
    ).astype(f32)
    denominator = full_dot(own, gram_first * gram_new, ((1,), (0,)))
    time_new = (own * time_sum / denominator).astype(jnp.bfloat16)
    time_new = double(time_new, "ja", size_j, 1)
    first_out = first_new.T
    return (first_out, second_new, time_new)


def in_layer(sizes, *args):
    return on_device(*sizes, *args)


def solution(mesh):
    sizes = (mesh.shape["ia"], mesh.shape["ja"], mesh.shape["ka"])
    return jax.shard_map(
        functools.partial(in_layer, sizes),
        mesh=mesh,
        in_specs=(
            P("ia", "ja", "ka"),
            P(None, ("ia", "ja", "ka")),
            P("ia", None),
            P("ja", None),
            P("ka", None),
            P(("ia", "ja", "ka"), None),
        ),
        out_specs=(P("ia", None), P("ja", None), P("ka", None)),
        check_vma=False,
    )
```
